32 devices in a mesh: mode: 16 (over z, x, core), space: 2 (over y).
Axes of the slice: x: 2, y: 2, z: 4, core: 2. Of those that a mesh axis runs over, the one named last changes fastest.
Arguments:
- forward_fields: float32 [2, 48, 512, 512], P(None, 'mode', 'space'), may hold values from -30 to 30
- backward_fields: float32 [2, 48, 512, 512], P(None, 'mode', 'space'), may hold values from -30 to 30
- phase: float32 [512, 512], P('space'), may hold values from -3.140625 to 3.140625
Outputs:
- new_phase: float32 [512, 512], P('space')
The draws below stay inside these ranges and needn't reach their ends.
All inputs are finite; a program needn't handle non-finite values.
Results may differ from the reference program's by a relative error of at most 0.0003.
Values sent between devices are 32-bit elements; how exact they have to be, the bound alone decides.
No kernel may reach another device: no remote copies, remote signals or barrier semaphores. Data moves between devices by JAX's collectives and lax.ppermute only.
A program may use at most 128 MiB of HBM per device.

```python
import math
import jax
import jax.numpy as jnp
from jax import lax

PIX = 512
MODES = 48


def field_draw(key, fold_value):
    mixed_key = jax.random.fold_in(key, fold_value)
    noise_key, row_key, col_key = jax.random.split(mixed_key, 3)
    full_shape = (2, MODES, PIX, PIX)
    noise = jnp.clip(jax.random.normal(noise_key, full_shape, jnp.float32), -4.0, 4.0)
    spread = math.log(3.2)
    rising = 0.6 * jnp.arange(PIX, dtype=jnp.float32)[None, :] / PIX
    row_scale = jnp.exp(spread * jax.random.uniform(row_key, (MODES, PIX), jnp.float32) + rising)
    col_scale = jnp.exp(spread * jax.random.uniform(col_key, (MODES, PIX), jnp.float32))
    return 0.2 * noise * row_scale[None, :, :, None] * col_scale[None, :, None, :]


def draw_forward_fields(key, part):
    return field_draw(key, 11)


def draw_backward_fields(key, part):
    return field_draw(key, 23)


def setup_inputs(seed: int = 0) -> dict:
    key_of = jax.random.split(jax.random.key(seed), 4)
    return {
        "forward_fields": draw_forward_fields(jax.random.fold_in(key_of[3], 71), 0),
        "backward_fields": draw_backward_fields(jax.random.fold_in(key_of[3], 71), 0),
        "phase": jnp.clip(jax.random.uniform(key_of[2], (PIX, PIX), jnp.float32, -3.140625, 3.140625), -3.140625, 3.140625),
    }


gap_length = 0.02
wavelength = 1.55e-06
pixel_pitch = 8e-06

def transfer_phase(pixels):
    indices = jnp.arange(pixels, dtype=jnp.int32)
    signed = jnp.where(indices < pixels // 2, indices, indices - pixels).astype(jnp.float32)
    squared = signed[:, None] ** 2 + signed[None, :] ** 2
    scaled = squared * (wavelength / (pixels * pixel_pitch)) ** 2
    return -2.0 * math.pi * (gap_length / wavelength) * scaled / (1.0 + jnp.sqrt(1.0 - scaled))

def propagate(real_part, imag_part, angles, direction):
    complex_field = real_part + 1j * imag_part
    spectrum = jnp.fft.fft2(complex_field, axes=(-2, -1))
    factor = jnp.cos(angles) + 1j * direction * jnp.sin(angles)
    return jnp.fft.ifft2(spectrum * factor, axes=(-2, -1))

def reference(forward_fields, backward_fields, phase):
    angles = transfer_phase(PIX)
    arrived = propagate(forward_fields[0], forward_fields[1], angles, 1.0)
    returned = propagate(backward_fields[0], backward_fields[1], angles, -1.0)
    product = jnp.conj(returned) * arrived
    rotation = jnp.cos(phase) + 1j * jnp.sin(phase)
    correlation = lax.optimization_barrier(jnp.sum(product * rotation, axis=(1, 2))) / PIX
    power_sum = lax.optimization_barrier(jnp.sum(jnp.real(product) ** 2 + jnp.imag(product) ** 2, axis=(1, 2))) / (PIX * PIX)
    weight = jnp.conj(correlation) / jnp.sqrt(jnp.real(correlation) ** 2 + jnp.imag(correlation) ** 2 + power_sum + 1e-06)
    drive_field = lax.optimization_barrier(jnp.sum(weight[:, None, None] * product, axis=0)) / math.sqrt(MODES)
    turned = drive_field * rotation
    step_size = jnp.imag(turned) / jnp.sqrt(jnp.real(drive_field) ** 2 + jnp.imag(drive_field) ** 2 + 1.0)
    return (phase - step_size).astype(jnp.float32)
```

```python
import math

import jax
import jax.numpy as jnp
import numpy as np
from jax import lax
from jax.experimental import pallas as pl
from jax.experimental.pallas import tpu as pltpu
from jax.sharding import PartitionSpec as P

gap_length = 0.02
wavelength = 1.55e-06
pixel_pitch = 8e-06
highest = lax.Precision.HIGHEST


def fourier_tables(pixels):
    indices = jnp.arange(pixels, dtype=jnp.int32)
    wrapped = indices[:, None] * indices[None, :] % pixels
    angles = 2.0 * math.pi / pixels * wrapped.astype(jnp.float32)
    return jnp.concatenate([jnp.cos(angles), jnp.sin(angles)], axis=1)


def transfer_block(pixels, first_column, col_width):
    indices = jnp.arange(pixels, dtype=jnp.int32)
    signed_rows = jnp.where(indices < pixels // 2, indices, indices - pixels).astype(jnp.float32)
    columns = first_column + jnp.arange(col_width, dtype=jnp.int32)
    signed_cols = jnp.where(columns < pixels // 2, columns, columns - pixels).astype(jnp.float32)
    squared = signed_rows[None, :] ** 2 + signed_cols[:, None] ** 2
    scaled = squared * (wavelength / (pixels * pixel_pitch)) ** 2
    angles = -2.0 * math.pi * (gap_length / wavelength) * scaled / (1.0 + jnp.sqrt(1.0 - scaled))
    return (jnp.cos(angles), jnp.sin(angles))


def rows_forward(fields, kernel, blocks):
    pixels = kernel.shape[0]
    rows_here = fields.shape[3]
    from_real = jnp.einsum("dkrx,xf->dkfr", fields[0], kernel, precision=highest)
    from_imag = jnp.einsum("dkrx,xf->dkfr", fields[1], kernel, precision=highest)
    spec_real = from_real[:, :, :pixels] + from_imag[:, :, pixels:]
    spec_imag = from_imag[:, :, :pixels] - from_real[:, :, pixels:]
    stacked = jnp.stack([spec_real, spec_imag])
    return stacked.reshape(
        2, fields.shape[1], fields.shape[2], blocks, pixels // blocks * rows_here
    )


def columns_section(column_data, kernel, cos_part, sin_part, directions, blocks):
    pixels = kernel.shape[0]
    rows_here = pixels // blocks
    col_width = column_data.shape[4] // rows_here
    depth = column_data.shape[1]
    items = column_data.shape[2]
    arranged = column_data.reshape(2, depth, items, blocks, col_width, rows_here)
    folded = kernel.reshape(blocks, rows_here, 2 * pixels)
    from_real = jnp.einsum("dkncr,nrf->dkcf", arranged[0], folded, precision=highest)
    from_imag = jnp.einsum("dkncr,nrf->dkcf", arranged[1], folded, precision=highest)
    freq_real = from_real[..., :pixels] + from_imag[..., pixels:]
    freq_imag = from_imag[..., :pixels] - from_real[..., pixels:]
    turned_sin = directions[:, None, None, None] * sin_part[None, None]
    moved_real = freq_real * cos_part - freq_imag * turned_sin
    moved_imag = freq_real * turned_sin + freq_imag * cos_part
    inverse_kernel = kernel.reshape(pixels, 2, blocks, rows_here)
    from_real = jnp.einsum("dkca,agnr->dkgncr", moved_real, inverse_kernel, precision=highest)
    from_imag = jnp.einsum("dkca,agnr->dkgncr", moved_imag, inverse_kernel, precision=highest)
    out_real = (from_real[:, :, 0] - from_imag[:, :, 1]) / pixels
    out_imag = (from_imag[:, :, 0] + from_real[:, :, 1]) / pixels
    stacked = jnp.stack([out_real, out_imag])
    return stacked.reshape(2, depth, items, blocks, col_width * rows_here)


def rows_inverse(column_data, kernel, blocks):
    pixels = kernel.shape[0]
    col_width = pixels // blocks
    rows_here = column_data.shape[4] // col_width
    arranged = column_data.reshape(
        2, column_data.shape[1], column_data.shape[2], blocks, col_width, rows_here
    )
    folded = kernel.reshape(blocks, col_width, 2 * pixels)
    from_real = jnp.einsum("dkncr,ncf->dkrf", arranged[0], folded, precision=highest)
    from_imag = jnp.einsum("dkncr,ncf->dkrf", arranged[1], folded, precision=highest)
    out_real = (from_real[..., :pixels] - from_imag[..., pixels:]) / pixels
    out_imag = (from_imag[..., :pixels] + from_real[..., pixels:]) / pixels
    return jnp.stack([out_real, out_imag])


def propagate(fields, directions, to_columns, to_rows, kernel, cos_part, sin_part, blocks):
    spectrum = rows_forward(fields, kernel, blocks)

    def column_work(column_data):
        return columns_section(column_data, kernel, cos_part, sin_part, directions, blocks)

    mixed = to_columns(spectrum, column_work)
    return rows_inverse(to_rows(mixed), kernel, blocks)


def phase_update(drive_real, drive_imag, phase):
    turned_imag = drive_real * jnp.sin(phase) + drive_imag * jnp.cos(phase)
    return phase - turned_imag / jnp.sqrt(drive_real * drive_real + drive_imag * drive_imag + 1.0)


def split_planes(forward_fields, backward_fields, phase):
    blocks = lax.axis_size("space")
    pixels = forward_fields.shape[3]
    per_device = forward_fields.shape[1]
    col_width = pixels // blocks
    kernel = fourier_tables(pixels)
    cos_part, sin_part = transfer_block(pixels, lax.axis_index("space") * col_width, col_width)
    arrived = propagate(
        forward_fields[:, None],
        jnp.ones((1,), jnp.float32),
        lambda payload, worker: worker(
            lax.all_to_all(payload, "space", split_axis=3, concat_axis=3, tiled=True)
        ),
        lambda payload: lax.all_to_all(payload, "space", split_axis=3, concat_axis=3, tiled=True),
        kernel,
        cos_part,
        sin_part,
        blocks,
    )[:, 0]
    returned = propagate(
        backward_fields[:, None],
        -jnp.ones((1,), jnp.float32),
        lambda payload, worker: worker(
            lax.all_to_all(payload, "space", split_axis=3, concat_axis=3, tiled=True)
        ),
        lambda payload: lax.all_to_all(payload, "space", split_axis=3, concat_axis=3, tiled=True),
        kernel,
        cos_part,
        sin_part,
        blocks,
    )[:, 0]
    product_real = returned[0] * arrived[0] + returned[1] * arrived[1]
    product_imag = returned[0] * arrived[1] - returned[1] * arrived[0]
    rotor_cos = jnp.cos(phase)
    rotor_sin = jnp.sin(phase)
    turn_real = product_real * rotor_cos - product_imag * rotor_sin
    turn_imag = product_real * rotor_sin + product_imag * rotor_cos
    local_real = jnp.sum(turn_real, axis=(1, 2)) / pixels
    local_imag = jnp.sum(turn_imag, axis=(1, 2)) / pixels
    local_power = jnp.sum(
        product_real * product_real + product_imag * product_imag, axis=(1, 2)
    ) / (pixels * pixels)
    correlation_real, correlation_imag, power_sum = lax.psum(
        (local_real, local_imag, local_power), "space"
    )
    inverse_norm = 1.0 / jnp.sqrt(
        correlation_real * correlation_real
        + correlation_imag * correlation_imag
        + power_sum
        + 1e-06
    )
    weight_real = (correlation_real * inverse_norm)[:, None, None]
    weight_imag = (-correlation_imag * inverse_norm)[:, None, None]
    drive_real = jnp.sum(weight_real * product_real - weight_imag * product_imag, axis=0)
    drive_imag = jnp.sum(weight_real * product_imag + weight_imag * product_real, axis=0)
    mode_root = math.sqrt(per_device * lax.axis_size("mode"))
    total_real, total_imag = lax.psum((drive_real, drive_imag), "mode")
    return phase_update(total_real / mode_root, total_imag / mode_root, phase)


def split_table(pixels):
    half = pixels // 2
    grid = np.outer(np.arange(half), np.arange(half)) % half
    angle = 2.0 * np.pi / half * grid
    cos, sin = np.cos(angle), np.sin(angle)
    matrix = np.block([[cos, -sin], [sin, cos]]).astype(np.float32)
    high = matrix.astype(jnp.bfloat16)
    low = (matrix - high.astype(np.float32)).astype(jnp.bfloat16)
    return np.stack([high, low])


def halves(value):
    high = value.astype(jnp.bfloat16)
    return high, (value - high.astype(jnp.float32)).astype(jnp.bfloat16)


def right_times(value, table):
    high, low = halves(value)
    left = jnp.concatenate([high, high, low], axis=1)
    right = jnp.concatenate([table[0], table[1], table[0]], axis=0)
    return jnp.dot(left, right, preferred_element_type=jnp.float32)


def left_times(table, value):
    high, low = halves(value)
    left = jnp.concatenate([table[0], table[1], table[0]], axis=1)
    right = jnp.concatenate([high, high, low], axis=0)
    return jnp.dot(left, right, preferred_element_type=jnp.float32)


def turn_back(real, imag, cos, sin):
    return real * cos + imag * sin, imag * cos - real * sin


def rows_kernel(index, fields, matrix, turn, out):
    half = out.shape[3]
    rows = out.shape[2]
    real, imag = fields[0, 0], fields[1, 0]
    sum_r, sum_i = real[:, :half] + real[:, half:], imag[:, :half] + imag[:, half:]
    odd_r, odd_i = turn_back(
        real[:, :half] - real[:, half:], imag[:, :half] - imag[:, half:], turn[0:1, :], turn[1:2, :]
    )
    stacked = jnp.concatenate(
        [jnp.concatenate([sum_r, sum_i], axis=1), jnp.concatenate([odd_r, odd_i], axis=1)], axis=0
    )
    result = right_times(stacked, matrix)
    out[0, 0] = result[:rows, :half]
    out[0, 1] = result[:rows, half:]
    out[1, 0] = result[rows:, :half]
    out[1, 1] = result[rows:, half:]


def columns_part(own, other, matrix, turned, turn_in, turn_out, cos_part, sin_part, sign, mixed):
    own_r, own_i = own[0], own[1]
    other_r, other_i = other[0], other[1]
    half, cols = own_r.shape

    def spread(value):
        return jnp.concatenate([value] * (cols // value.shape[1]), axis=1)

    odd_r, odd_i = turn_back(
        own_r - other_r, own_i - other_i, spread(turn_in[0]), spread(turn_in[1])
    )
    stacked = jnp.concatenate(
        [
            jnp.concatenate([own_r + other_r, odd_r], axis=1),
            jnp.concatenate([own_i + other_i, odd_i], axis=1),
        ],
        axis=0,
    )
    freq = left_times(turned, stacked)
    freq_r, freq_i = freq[:half], freq[half:]
    tc = jnp.concatenate([cos_part[0], cos_part[1]], axis=1)
    ts = jnp.concatenate([sin_part[0], sin_part[1]], axis=1)
    if sign < 0:
        moved_r, moved_i = freq_r * tc + freq_i * ts, freq_i * tc - freq_r * ts
    else:
        moved_r, moved_i = freq_r * tc - freq_i * ts, freq_i * tc + freq_r * ts
    back = left_times(matrix, jnp.concatenate([moved_r, moved_i], axis=0))
    even_r, even_i = back[:half, :cols], back[half:, :cols]
    odd_r, odd_i = back[:half, cols:], back[half:, cols:]
    cos, sin = spread(turn_out[0]), spread(turn_out[1])
    add_r, add_i = odd_r * cos - odd_i * sin, odd_i * cos + odd_r * sin
    mixed[0, :half, :] = even_r + add_r
    mixed[1, :half, :] = even_i + add_i
    mixed[0, half:, :] = even_r - add_r
    mixed[1, half:, :] = even_i - add_i


def rows_back(mixed_even, mixed_odd, turned, turn, rows):
    stacked = jnp.concatenate(
        [
            jnp.concatenate([mixed_even[0, rows, :], mixed_even[1, rows, :]], axis=1),
            jnp.concatenate([mixed_odd[0, rows, :], mixed_odd[1, rows, :]], axis=1),
        ],
        axis=0,
    )
    back = right_times(stacked, turned)
    block = back.shape[0] // 2
    half = back.shape[1] // 2
    even_r, even_i = back[:block, :half], back[:block, half:]
    odd_r, odd_i = back[block:, :half], back[block:, half:]
    cos, sin = turn[0:1, :], turn[1:2, :]
    add_r, add_i = odd_r * cos - odd_i * sin, odd_i * cos + odd_r * sin
    return (
        jnp.concatenate([even_r + add_r, even_r - add_r], axis=1),
        jnp.concatenate([even_i + add_i, even_i - add_i], axis=1),
    )


BLOCK = 128


def product_part(arr_r, arr_i, returned, phase_turn, product, rows, sums):
    ret_r, ret_i = returned[0, rows, :], returned[1, rows, :]
    pro_r, pro_i = ret_r * arr_r + ret_i * arr_i, ret_r * arr_i - ret_i * arr_r
    product[0, rows, :] = pro_r
    product[1, rows, :] = pro_i
    cos, sin = phase_turn[0, rows, :], phase_turn[1, rows, :]

    def fold(value):
        return jnp.sum(value.reshape(value.shape[0] // 8, 8, value.shape[1]), axis=0)

    return (
        sums[0] + fold(pro_r * cos - pro_i * sin),
        sums[1] + fold(pro_r * sin + pro_i * cos),
        sums[2] + fold(pro_r * pro_r + pro_i * pro_i),
    )


def weight_of(sums, pixels):
    def total(value):
        return jnp.sum(jnp.sum(value, axis=0, keepdims=True), axis=1, keepdims=True)

    cor_r, cor_i = total(sums[0]) / pixels, total(sums[1]) / pixels
    power = total(sums[2]) / (pixels * pixels)
    norm = 1.0 / jnp.sqrt(cor_r * cor_r + cor_i * cor_i + power + 1e-06)
    return cor_r * norm, -cor_i * norm


def back_kernel(own, other, matrix, turned, turn, turn_in, turn_out, cos_part, sin_part, out, mixed):
    for e in range(2):
        columns_part(
            own.at[e], other.at[e], matrix, turned, turn_in, turn_out,
            cos_part.at[e], sin_part.at[e], -1, mixed.at[e],
        )

    def step(i, carry):
        rows = pl.ds(pl.multiple_of(i * BLOCK, BLOCK), BLOCK)
        real, imag = rows_back(mixed.at[0], mixed.at[1], turned, turn, rows)
        out[0, rows, :] = real
        out[1, rows, :] = imag
        return carry

    lax.fori_loop(0, out.shape[1] // BLOCK, step, 0)


def columns_kernel(own, other, matrix, turned, turn_in, turn_out, cos_part, sin_part, mixed):
    columns_part(
        own, other, matrix, turned, turn_in, turn_out, cos_part, sin_part, 1, mixed
    )


def last_kernel(
    flag, own, other, mixed_even, returned, phase_turn,
    matrix, turned, turn, turn_in, turn_out, cos_part, sin_part, out, mixed, product,
):
    pixels = returned.shape[1]
    columns_part(
        own, other, matrix, turned, turn_in, turn_out, cos_part, sin_part, 1, mixed
    )

    def step(i, sums):
        rows = pl.ds(pl.multiple_of(i * BLOCK, BLOCK), BLOCK)
        real, imag = rows_back(mixed_even, mixed, turned, turn, rows)
        return product_part(real, imag, returned, phase_turn, product, rows, sums)

    zero = jnp.zeros((8, pixels), jnp.float32)
    sums = lax.fori_loop(0, pixels // BLOCK, step, (zero, zero, zero))
    weight_r, weight_i = weight_of(sums, pixels)
    weight_r, weight_i = weight_r * flag[0], weight_i * flag[0]

    def apply(i, carry):
        rows = pl.ds(pl.multiple_of(i * 32, 32), 32)
        pro_r, pro_i = product[0, rows, :], product[1, rows, :]
        out[0, rows, :] = weight_r * pro_r - weight_i * pro_i
        out[1, rows, :] = weight_r * pro_i + weight_i * pro_r
        return carry

    lax.fori_loop(0, pixels // 32, apply, 0)


def final_kernel(
    place, own, other, mixed_even, returned, phase_turn, drive,
    matrix, turned, turn, turn_in, turn_out, cos_part, sin_part, kept, sent, mixed, product,
):
    pixels = returned.shape[1]
    columns_part(
        own, other, matrix, turned, turn_in, turn_out, cos_part, sin_part, 1, mixed
    )

    def step(i, sums):
        rows = pl.ds(pl.multiple_of(i * BLOCK, BLOCK), BLOCK)
        real, imag = rows_back(mixed_even, mixed, turned, turn, rows)
        return product_part(real, imag, returned, phase_turn, product, rows, sums)

    zero = jnp.zeros((8, pixels), jnp.float32)
    sums = lax.fori_loop(0, pixels // BLOCK, step, (zero, zero, zero))
    weight_r, weight_i = weight_of(sums, pixels)
    part = pixels // 4

    for out, core in ((sent, 1 - place[0]), (kept, place[0])):
        for s in range(2):

            def apply(i, carry, s=s, out=out, core=core):
                rows = pl.ds(pl.multiple_of((2 * s + core) * part + i * 32, 32), 32)
                to = pl.ds(pl.multiple_of(i * 32, 32), 32)
                pro_r, pro_i = product[0, rows, :], product[1, rows, :]
                out[0, s, to, :] = drive[0, rows, :] + (weight_r * pro_r - weight_i * pro_i)
                out[1, s, to, :] = drive[1, rows, :] + (weight_r * pro_i + weight_i * pro_r)
                return carry

            lax.fori_loop(0, part // 32, apply, 0)


def in_vmem(count):
    return [pl.BlockSpec(memory_space=pltpu.VMEM) for _ in range(count)]


def in_smem():
    return pl.BlockSpec(memory_space=pltpu.SMEM)


def limit(mebibytes):
    return pltpu.CompilerParams(vmem_limit_bytes=mebibytes * 1024 * 1024)


def rows_call(index, fields, matrix, turn):
    _, _, rows, pixels = fields.shape
    block = rows // 2
    return pl.pallas_call(
        rows_kernel,
        out_shape=jax.ShapeDtypeStruct((2, 2, rows, pixels // 2), jnp.float32),
        grid_spec=pltpu.PrefetchScalarGridSpec(
            num_scalar_prefetch=1,
            grid=(rows // block,),
            in_specs=[
                pl.BlockSpec((2, 1, block, pixels), lambda i, index: (0, index[0], i, 0)),
                pl.BlockSpec(memory_space=pltpu.VMEM),
                pl.BlockSpec(memory_space=pltpu.VMEM),
            ],
            out_specs=pl.BlockSpec((2, 2, block, pixels // 2), lambda i, index: (0, 0, i, 0)),
        ),
        compiler_params=limit(ROWS_LIMIT),
        name="rows",
    )(index.reshape(1), fields, matrix, turn)


ROWS_LIMIT = 16
FIELD_LIMIT = 30


def back_call(own, other, tables):
    half = own.shape[2]
    return pl.pallas_call(
        back_kernel,
        out_shape=jax.ShapeDtypeStruct((2, 2 * half, 2 * half), jnp.float32),
        in_specs=in_vmem(9),
        out_specs=in_vmem(1)[0],
        scratch_shapes=[pltpu.VMEM((2, 2, 2 * half, half), jnp.float32)],
        compiler_params=limit(FIELD_LIMIT),
        name="back",
    )(own, other, tables["matrix"], tables["turned"], tables["turn"], tables["turn_in"],
      tables["turn_out"], tables["cos"], tables["sin"])


def columns_call(own, other, tables, e):
    half = own.shape[1]
    return pl.pallas_call(
        columns_kernel,
        out_shape=jax.ShapeDtypeStruct((2, 2 * half, half), jnp.float32),
        in_specs=in_vmem(8),
        out_specs=in_vmem(1)[0],
        compiler_params=limit(FIELD_LIMIT),
        name="columns",
    )(own, other, tables["matrix"], tables["turned"], tables["turn_in"],
      tables["turn_out"], tables["cos"][e], tables["sin"][e])


def last_call(flag, own, other, mixed_even, returned, phase_turn, tables):
    pixels = returned.shape[1]
    return pl.pallas_call(
        last_kernel,
        out_shape=jax.ShapeDtypeStruct(returned.shape, jnp.float32),
        in_specs=[in_smem()] + in_vmem(12),
        out_specs=in_vmem(1)[0],
        scratch_shapes=[pltpu.VMEM(mixed_even.shape, jnp.float32), pltpu.VMEM(returned.shape, jnp.float32)],
        compiler_params=limit(FIELD_LIMIT),
        name="last",
    )(flag.reshape(1), own, other, mixed_even, returned, phase_turn, tables["matrix"], tables["turned"],
      tables["turn"], tables["turn_in"], tables["turn_out"], tables["cos"][1], tables["sin"][1])


def final_call(place, own, other, mixed_even, returned, phase_turn, drive, tables):
    pixels = returned.shape[1]
    part = jax.ShapeDtypeStruct((2, 2, pixels // 4, pixels), jnp.float32)
    return pl.pallas_call(
        final_kernel,
        out_shape=(part, part),
        in_specs=[in_smem()] + in_vmem(13),
        out_specs=tuple(in_vmem(2)),
        scratch_shapes=[pltpu.VMEM(mixed_even.shape, jnp.float32), pltpu.VMEM(returned.shape, jnp.float32)],
        compiler_params=limit(FIELD_LIMIT),
        name="final",
    )(place.reshape(1), own, other, mixed_even, returned, phase_turn, drive, tables["matrix"], tables["turned"],
      tables["turn"], tables["turn_in"], tables["turn_out"], tables["cos"][1], tables["sin"][1])


def permuted_transfer(pixels):
    half = pixels // 2
    order = jnp.arange(2, dtype=jnp.int32)[:, None] + 2 * jnp.arange(half, dtype=jnp.int32)[None, :]
    signed = jnp.where(order < half, order, order - pixels).astype(jnp.float32)
    cos_parts, sin_parts = [], []
    for e in range(2):
        squared = signed[:, :, None] ** 2 + signed[e][None, None, :] ** 2
        scaled = squared * (wavelength / (pixels * pixel_pitch)) ** 2
        angles = -2.0 * math.pi * (gap_length / wavelength) * scaled / (1.0 + jnp.sqrt(1.0 - scaled))
        cos_parts.append(jnp.cos(angles) / (pixels * pixels))
        sin_parts.append(jnp.sin(angles) / (pixels * pixels))
    return cos_parts, sin_parts


def after(value, *others):
    return lax.optimization_barrier((value,) + others)[0]


def whole_modes(forward_fields, backward_fields, phase):
    pixels = forward_fields.shape[3]
    half = pixels // 2
    modes_here = forward_fields.shape[1]
    mode_size = lax.axis_size("mode")
    outer = mode_size // 4
    axes = ("mode", "space")
    mode_index = lax.axis_index("mode")
    space_index = lax.axis_index("space")
    core_index = mode_index % 2
    x_index = mode_index // 2 % 2
    z_index = mode_index // 4

    def flat(mode, space):
        return mode * 2 + space

    everyone = [(mode, space) for mode in range(mode_size) for space in range(2)]
    to_space = [(flat(m, s), flat(m, 1 - s)) for m, s in everyone]
    to_core = [(flat(m, s), flat(m ^ 1, s)) for m, s in everyone]
    to_x = [(flat(m, s), flat(m ^ 2, s)) for m, s in everyone]
    to_z = {j: [(flat(m, s), flat(m ^ (4 * j), s)) for m, s in everyone] for j in range(1, outer)}
    last_mode = [(flat(m, 1 - m % 2), flat(m, m % 2)) for m in range(mode_size)]

    def send(value, pairs):
        return lax.ppermute(value, axes, pairs)

    def swap_if(bit, value):
        return jnp.where(bit == 1, value[::-1], value)

    def by_z(value):
        shape = value.shape
        value = value.reshape((outer // 2, 2) + shape[1:])
        value = jnp.where(z_index % 2 == 1, value[:, ::-1], value)
        value = swap_if(z_index // 2, value)
        return value.reshape(shape)

    piece_rows = half // mode_size
    place = (core_index * 2 + x_index) * outer + z_index
    piece = lax.dynamic_slice_in_dim(phase, place * piece_rows, piece_rows, axis=0)

    def gather(piece):
        pieces = by_z(jnp.stack([piece] + [send(piece, to_z[j]) for j in range(1, outer)]))
        pieces = swap_if(x_index, jnp.stack([pieces, send(pieces, to_x)]))
        pieces = swap_if(core_index, jnp.stack([pieces, send(pieces, to_core)]))
        return pieces.reshape(half, pixels)

    matrix = jnp.asarray(split_table(pixels))
    angle = 2.0 * np.pi / pixels * np.arange(half)
    turn = jnp.asarray(np.stack([np.cos(angle), np.sin(angle)]).astype(np.float32))

    other_piece = send(piece, to_space)
    last = jnp.full((), modes_here - 1, jnp.int32)
    rows_last_backward = rows_call(after(last, piece), backward_fields, matrix, turn)
    got_last_backward = send(rows_last_backward, last_mode)
    rows_last_forward = rows_call(after(last, rows_last_backward), forward_fields, matrix, turn)
    got_last_even = send(rows_last_forward[0], last_mode)
    got_last_odd = send(rows_last_forward[1], last_mode)
    sent_backward = rows_call(after(1 - space_index, rows_last_forward), backward_fields, matrix, turn)
    got_backward = send(sent_backward, to_space)
    sent_forward = rows_call(after(1 - space_index, sent_backward), forward_fields, matrix, turn)
    got_even = send(sent_forward[0], to_space)
    got_odd = send(sent_forward[1], to_space)
    own_backward = rows_call(after(space_index, sent_forward), backward_fields, matrix, turn)
    own_forward = rows_call(after(space_index, own_backward), forward_fields, matrix, turn)

    other_phase = gather(other_piece)
    whole_phase = swap_if(space_index, jnp.stack([phase, other_phase])).reshape(pixels, pixels)
    phase_turn = jnp.stack([jnp.cos(whole_phase), jnp.sin(whole_phase)])

    turn_out = jnp.broadcast_to(turn[:, :, None], (2, half, 128))
    cos_parts, sin_parts = permuted_transfer(pixels)
    tables = {
        "matrix": matrix,
        "turned": lax.optimization_barrier(matrix).transpose(0, 2, 1),
        "turn": turn,
        "turn_out": turn_out,
        "turn_in": turn_out * (1.0 - 2.0 * space_index.astype(jnp.float32)),
        "cos": cos_parts,
        "sin": sin_parts,
    }
    joined = dict(tables, cos=jnp.stack(cos_parts), sin=jnp.stack(sin_parts))

    takes_last = jnp.where(space_index == core_index, 1.0, 0.0)
    returned = back_call(rows_last_backward, got_last_backward, joined)
    mixed_even = columns_call(after(rows_last_forward[0], returned), got_last_even, tables, 0)
    drive = last_call(
        takes_last, rows_last_forward[1], got_last_odd, mixed_even, returned, phase_turn, tables
    )
    returned = back_call(after(own_backward, drive), got_backward, joined)
    mixed_even = columns_call(after(own_forward[0], returned), got_even, tables, 0)
    kept, sent = final_call(
        core_index, own_forward[1], got_odd, mixed_even, returned, phase_turn, drive, tables
    )
    drive = kept + send(sent, to_core)

    drive = drive.reshape(2, 2, 2, outer, piece_rows, pixels)

    def keep(value, axis, index):
        return lax.dynamic_index_in_dim(value, index, axis=axis, keepdims=False)

    def step(value, axis, index, pairs):
        return keep(value, axis, index) + send(keep(value, axis, 1 - index), pairs)

    real = step(drive[0], 1, x_index, to_x)
    imag = step(drive[1], 0, space_index, to_space)
    real = step(real, 0, space_index, to_space)
    imag = step(imag, 0, x_index, to_x)
    both = by_z(jnp.stack([real, imag], axis=1))
    total = both[0]
    for j in range(1, outer):
        total = total + send(both[j], to_z[j])
    mode_root = math.sqrt(modes_here * mode_size)
    updated = phase_update(total[0] / mode_root, total[1] / mode_root, piece)
    return gather(updated)


def on_device(forward_fields, backward_fields, phase):
    pixels = forward_fields.shape[3]
    if (
        lax.axis_size("space") == 2
        and lax.axis_size("mode") == 16
        and forward_fields.shape[1] == 3
        and pixels % 512 == 0
    ):
        return whole_modes(forward_fields, backward_fields, phase)
    return split_planes(forward_fields, backward_fields, phase)


def solution(mesh):
    in_specs = (P(None, "mode", "space", None), P(None, "mode", "space", None), P("space", None))
    out_specs = P("space", None)
    return jax.shard_map(
        on_device, mesh=mesh, in_specs=in_specs, out_specs=out_specs, check_vma=False
    )
```

```python
import math

import jax
import jax.numpy as jnp
import numpy as np
from jax import lax
from jax.experimental import pallas as pl
from jax.experimental.pallas import tpu as pltpu
from jax.sharding import PartitionSpec as P

gap_length = 0.02
wavelength = 1.55e-06
pixel_pitch = 8e-06
highest = lax.Precision.HIGHEST


def fourier_tables(pixels):
    indices = jnp.arange(pixels, dtype=jnp.int32)
    wrapped = indices[:, None] * indices[None, :] % pixels
    angles = 2.0 * math.pi / pixels * wrapped.astype(jnp.float32)
    return jnp.concatenate([jnp.cos(angles), jnp.sin(angles)], axis=1)


def transfer_block(pixels, first_column, col_width):
    indices = jnp.arange(pixels, dtype=jnp.int32)
    signed_rows = jnp.where(indices < pixels // 2, indices, indices - pixels).astype(jnp.float32)
    columns = first_column + jnp.arange(col_width, dtype=jnp.int32)
    signed_cols = jnp.where(columns < pixels // 2, columns, columns - pixels).astype(jnp.float32)
    squared = signed_rows[None, :] ** 2 + signed_cols[:, None] ** 2
    scaled = squared * (wavelength / (pixels * pixel_pitch)) ** 2
    angles = -2.0 * math.pi * (gap_length / wavelength) * scaled / (1.0 + jnp.sqrt(1.0 - scaled))
    return (jnp.cos(angles), jnp.sin(angles))


def rows_forward(fields, kernel, blocks):
    pixels = kernel.shape[0]
    rows_here = fields.shape[3]
    from_real = jnp.einsum("dkrx,xf->dkfr", fields[0], kernel, precision=highest)
    from_imag = jnp.einsum("dkrx,xf->dkfr", fields[1], kernel, precision=highest)
    spec_real = from_real[:, :, :pixels] + from_imag[:, :, pixels:]
    spec_imag = from_imag[:, :, :pixels] - from_real[:, :, pixels:]
    stacked = jnp.stack([spec_real, spec_imag])
    return stacked.reshape(
        2, fields.shape[1], fields.shape[2], blocks, pixels // blocks * rows_here
    )


def columns_section(column_data, kernel, cos_part, sin_part, directions, blocks):
    pixels = kernel.shape[0]
    rows_here = pixels // blocks
    col_width = column_data.shape[4] // rows_here
    depth = column_data.shape[1]
    items = column_data.shape[2]
    arranged = column_data.reshape(2, depth, items, blocks, col_width, rows_here)
    folded = kernel.reshape(blocks, rows_here, 2 * pixels)
    from_real = jnp.einsum("dkncr,nrf->dkcf", arranged[0], folded, precision=highest)
    from_imag = jnp.einsum("dkncr,nrf->dkcf", arranged[1], folded, precision=highest)
    freq_real = from_real[..., :pixels] + from_imag[..., pixels:]
    freq_imag = from_imag[..., :pixels] - from_real[..., pixels:]
    turned_sin = directions[:, None, None, None] * sin_part[None, None]
    moved_real = freq_real * cos_part - freq_imag * turned_sin
    moved_imag = freq_real * turned_sin + freq_imag * cos_part
    inverse_kernel = kernel.reshape(pixels, 2, blocks, rows_here)
    from_real = jnp.einsum("dkca,agnr->dkgncr", moved_real, inverse_kernel, precision=highest)
    from_imag = jnp.einsum("dkca,agnr->dkgncr", moved_imag, inverse_kernel, precision=highest)
    out_real = (from_real[:, :, 0] - from_imag[:, :, 1]) / pixels
    out_imag = (from_imag[:, :, 0] + from_real[:, :, 1]) / pixels
    stacked = jnp.stack([out_real, out_imag])
    return stacked.reshape(2, depth, items, blocks, col_width * rows_here)


def rows_inverse(column_data, kernel, blocks):
    pixels = kernel.shape[0]
    col_width = pixels // blocks
    rows_here = column_data.shape[4] // col_width
    arranged = column_data.reshape(
        2, column_data.shape[1], column_data.shape[2], blocks, col_width, rows_here
    )
    folded = kernel.reshape(blocks, col_width, 2 * pixels)
    from_real = jnp.einsum("dkncr,ncf->dkrf", arranged[0], folded, precision=highest)
    from_imag = jnp.einsum("dkncr,ncf->dkrf", arranged[1], folded, precision=highest)
    out_real = (from_real[..., :pixels] - from_imag[..., pixels:]) / pixels
    out_imag = (from_imag[..., :pixels] + from_real[..., pixels:]) / pixels
    return jnp.stack([out_real, out_imag])


def propagate(fields, directions, to_columns, to_rows, kernel, cos_part, sin_part, blocks):
    spectrum = rows_forward(fields, kernel, blocks)

    def column_work(column_data):
        return columns_section(column_data, kernel, cos_part, sin_part, directions, blocks)

    mixed = to_columns(spectrum, column_work)
    return rows_inverse(to_rows(mixed), kernel, blocks)


def phase_update(drive_real, drive_imag, phase):
    turned_imag = drive_real * jnp.sin(phase) + drive_imag * jnp.cos(phase)
    return phase - turned_imag / jnp.sqrt(drive_real * drive_real + drive_imag * drive_imag + 1.0)


def split_planes(forward_fields, backward_fields, phase):
    blocks = lax.axis_size("space")
    pixels = forward_fields.shape[3]
    per_device = forward_fields.shape[1]
    col_width = pixels // blocks
    kernel = fourier_tables(pixels)
    cos_part, sin_part = transfer_block(pixels, lax.axis_index("space") * col_width, col_width)
    arrived = propagate(
        forward_fields[:, None],
        jnp.ones((1,), jnp.float32),
        lambda payload, worker: worker(
            lax.all_to_all(payload, "space", split_axis=3, concat_axis=3, tiled=True)
        ),
        lambda payload: lax.all_to_all(payload, "space", split_axis=3, concat_axis=3, tiled=True),
        kernel,
        cos_part,
        sin_part,
        blocks,
    )[:, 0]
    returned = propagate(
        backward_fields[:, None],
        -jnp.ones((1,), jnp.float32),
        lambda payload, worker: worker(
            lax.all_to_all(payload, "space", split_axis=3, concat_axis=3, tiled=True)
        ),
        lambda payload: lax.all_to_all(payload, "space", split_axis=3, concat_axis=3, tiled=True),
        kernel,
        cos_part,
        sin_part,
        blocks,
    )[:, 0]
    product_real = returned[0] * arrived[0] + returned[1] * arrived[1]
    product_imag = returned[0] * arrived[1] - returned[1] * arrived[0]
    rotor_cos = jnp.cos(phase)
    rotor_sin = jnp.sin(phase)
    turn_real = product_real * rotor_cos - product_imag * rotor_sin
    turn_imag = product_real * rotor_sin + product_imag * rotor_cos
    local_real = jnp.sum(turn_real, axis=(1, 2)) / pixels
    local_imag = jnp.sum(turn_imag, axis=(1, 2)) / pixels
    local_power = jnp.sum(
        product_real * product_real + product_imag * product_imag, axis=(1, 2)
    ) / (pixels * pixels)
    correlation_real, correlation_imag, power_sum = lax.psum(
        (local_real, local_imag, local_power), "space"
    )
    inverse_norm = 1.0 / jnp.sqrt(
        correlation_real * correlation_real
        + correlation_imag * correlation_imag
        + power_sum
        + 1e-06
    )
    weight_real = (correlation_real * inverse_norm)[:, None, None]
    weight_imag = (-correlation_imag * inverse_norm)[:, None, None]
    drive_real = jnp.sum(weight_real * product_real - weight_imag * product_imag, axis=0)
    drive_imag = jnp.sum(weight_real * product_imag + weight_imag * product_real, axis=0)
    mode_root = math.sqrt(per_device * lax.axis_size("mode"))
    total_real, total_imag = lax.psum((drive_real, drive_imag), "mode")
    return phase_update(total_real / mode_root, total_imag / mode_root, phase)


def split_table(pixels):
    half = pixels // 2
    grid = np.outer(np.arange(half), np.arange(half)) % half
    angle = 2.0 * np.pi / half * grid
    cos, sin = np.cos(angle), np.sin(angle)
    matrix = np.block([[cos, -sin], [sin, cos]]).astype(np.float32)
    high = matrix.astype(jnp.bfloat16)
    low = (matrix - high.astype(np.float32)).astype(jnp.bfloat16)
    return np.stack([high, low])


def halves(value):
    high = value.astype(jnp.bfloat16)
    return high, (value - high.astype(jnp.float32)).astype(jnp.bfloat16)


def right_times(value, table):
    high, low = halves(value)
    left = jnp.concatenate([high, high, low], axis=1)
    right = jnp.concatenate([table[0], table[1], table[0]], axis=0)
    return jnp.dot(left, right, preferred_element_type=jnp.float32)


def left_times(table, value):
    high, low = halves(value)
    left = jnp.concatenate([table[0], table[1], table[0]], axis=1)
    right = jnp.concatenate([high, high, low], axis=0)
    return jnp.dot(left, right, preferred_element_type=jnp.float32)


def turn_back(real, imag, cos, sin):
    return real * cos + imag * sin, imag * cos - real * sin


def rows_kernel(plan, brought, index, matrix, turn, held, sems):
    rows = held.shape[2]
    blocks = plan[0][0].shape[2] // rows
    half = held.shape[3] // 2
    copies = [
        pltpu.make_async_copy(
            fields.at[:, index[at], pl.ds(i * rows, rows), :],
            held.at[n * blocks + i],
            sems.at[n * blocks + i],
        )
        for n, (fields, at, _, _) in enumerate(plan)
        for i in range(blocks)
    ]
    copies[0].start()
    for copy in brought:
        copy.start()
    for copy in copies[1:]:
        copy.start()
    for n, (_, _, even, odd) in enumerate(plan):
        for i in range(blocks):
            copies[n * blocks + i].wait()
            if n == 0 and i == 0:
                for copy in brought:
                    copy.wait()
            real, imag = held[n * blocks + i, 0], held[n * blocks + i, 1]
            sum_r, sum_i = real[:, :half] + real[:, half:], imag[:, :half] + imag[:, half:]
            odd_r, odd_i = turn_back(
                real[:, :half] - real[:, half:],
                imag[:, :half] - imag[:, half:],
                turn[0:1, :],
                turn[1:2, :],
            )
            stacked = jnp.concatenate(
                [
                    jnp.concatenate([sum_r, sum_i], axis=1),
                    jnp.concatenate([odd_r, odd_i], axis=1),
                ],
                axis=0,
            )
            result = right_times(stacked, matrix)
            to = pl.ds(i * rows, rows)
            even[0, to, :] = result[:rows, :half]
            even[1, to, :] = result[:rows, half:]
            odd[0, to, :] = result[rows:, :half]
            odd[1, to, :] = result[rows:, half:]


def columns_part(own, other, matrix, turned, turn_in, turn_out, cos_part, sin_part, sign, mixed):
    own_r, own_i = own[0], own[1]
    other_r, other_i = other[0], other[1]
    half, cols = own_r.shape

    def spread(value):
        return jnp.concatenate([value] * (cols // value.shape[1]), axis=1)

    odd_r, odd_i = turn_back(
        own_r - other_r, own_i - other_i, spread(turn_in[0]), spread(turn_in[1])
    )
    stacked = jnp.concatenate(
        [
            jnp.concatenate([own_r + other_r, odd_r], axis=1),
            jnp.concatenate([own_i + other_i, odd_i], axis=1),
        ],
        axis=0,
    )
    freq = left_times(turned, stacked)
    freq_r, freq_i = freq[:half], freq[half:]
    tc = jnp.concatenate([cos_part[0], cos_part[1]], axis=1)
    ts = jnp.concatenate([sin_part[0], sin_part[1]], axis=1)
    if sign < 0:
        moved_r, moved_i = freq_r * tc + freq_i * ts, freq_i * tc - freq_r * ts
    else:
        moved_r, moved_i = freq_r * tc - freq_i * ts, freq_i * tc + freq_r * ts
    back = left_times(matrix, jnp.concatenate([moved_r, moved_i], axis=0))
    even_r, even_i = back[:half, :cols], back[half:, :cols]
    odd_r, odd_i = back[:half, cols:], back[half:, cols:]
    cos, sin = spread(turn_out[0]), spread(turn_out[1])
    add_r, add_i = odd_r * cos - odd_i * sin, odd_i * cos + odd_r * sin
    mixed[0, :half, :] = even_r + add_r
    mixed[1, :half, :] = even_i + add_i
    mixed[0, half:, :] = even_r - add_r
    mixed[1, half:, :] = even_i - add_i


def rows_back(mixed_even, mixed_odd, turned, turn, rows):
    stacked = jnp.concatenate(
        [
            jnp.concatenate([mixed_even[0, rows, :], mixed_even[1, rows, :]], axis=1),
            jnp.concatenate([mixed_odd[0, rows, :], mixed_odd[1, rows, :]], axis=1),
        ],
        axis=0,
    )
    back = right_times(stacked, turned)
    block = back.shape[0] // 2
    half = back.shape[1] // 2
    even_r, even_i = back[:block, :half], back[:block, half:]
    odd_r, odd_i = back[block:, :half], back[block:, half:]
    cos, sin = turn[0:1, :], turn[1:2, :]
    add_r, add_i = odd_r * cos - odd_i * sin, odd_i * cos + odd_r * sin
    return (
        jnp.concatenate([even_r + add_r, even_r - add_r], axis=1),
        jnp.concatenate([even_i + add_i, even_i - add_i], axis=1),
    )


BLOCK = 128
WIDE = 256


def product_part(arr_r, arr_i, returned, phase_turn, product, rows, sums):
    ret_r, ret_i = returned[0, rows, :], returned[1, rows, :]
    pro_r, pro_i = ret_r * arr_r + ret_i * arr_i, ret_r * arr_i - ret_i * arr_r
    product[0, rows, :] = pro_r
    product[1, rows, :] = pro_i
    cos, sin = phase_turn[0, rows, :], phase_turn[1, rows, :]

    def fold(value):
        return jnp.sum(value.reshape(value.shape[0] // 8, 8, value.shape[1]), axis=0)

    return (
        sums[0] + fold(pro_r * cos - pro_i * sin),
        sums[1] + fold(pro_r * sin + pro_i * cos),
        sums[2] + fold(pro_r * pro_r + pro_i * pro_i),
    )


def weight_of(sums, pixels):
    def total(value):
        return jnp.sum(jnp.sum(value, axis=0, keepdims=True), axis=1, keepdims=True)

    cor_r, cor_i = total(sums[0]) / pixels, total(sums[1]) / pixels
    power = total(sums[2]) / (pixels * pixels)
    norm = 1.0 / jnp.sqrt(cor_r * cor_r + cor_i * cor_i + power + 1e-06)
    return cor_r * norm, -cor_i * norm


def back_kernel(
    own, other, matrix, turned, turn, turn_in, turn_out, cos_even, sin_even, cos_odd, sin_odd, out, mixed
):
    for e, (cos_part, sin_part) in enumerate(((cos_even, sin_even), (cos_odd, sin_odd))):
        columns_part(
            own.at[e], other.at[e], matrix, turned, turn_in, turn_out,
            cos_part, sin_part, -1, mixed.at[e],
        )

    def step(i, carry):
        rows = pl.ds(pl.multiple_of(i * BLOCK, BLOCK), BLOCK)
        real, imag = rows_back(mixed.at[0], mixed.at[1], turned, turn, rows)
        out[0, rows, :] = real
        out[1, rows, :] = imag
        return carry

    lax.fori_loop(0, out.shape[1] // BLOCK, step, 0)


def even_kernel(own, other, matrix, turned, turn_in, turn_out, cos_part, sin_part, out, mixed):
    columns_part(
        own, other, matrix, turned, turn_in, turn_out, cos_part, sin_part, 1, mixed
    )
    half = out.shape[2]
    for i in range(out.shape[1] // WIDE):
        rows = pl.ds(i * WIDE, WIDE)
        back = right_times(jnp.concatenate([mixed[0, rows, :], mixed[1, rows, :]], axis=1), turned)
        out[0, rows, :] = back[:, :half]
        out[1, rows, :] = back[:, half:]


def even_and_odd(even, mixed, turned, turn, rows):
    half = even.shape[2]
    back = right_times(jnp.concatenate([mixed[0, rows, :], mixed[1, rows, :]], axis=1), turned)
    odd_r, odd_i = back[:, :half], back[:, half:]
    cos, sin = turn[0:1, :], turn[1:2, :]
    add_r, add_i = odd_r * cos - odd_i * sin, odd_i * cos + odd_r * sin
    even_r, even_i = even[0, rows, :], even[1, rows, :]
    return (
        jnp.concatenate([even_r + add_r, even_r - add_r], axis=1),
        jnp.concatenate([even_i + add_i, even_i - add_i], axis=1),
    )


def last_kernel(
    flag, own, other, returned, phase_turn, matrix, turned, turn, turn_in, turn_out,
    cos_even, sin_even, cos_odd, sin_odd, out, mixed, product,
):
    pixels = returned.shape[1]
    for e, (cos_part, sin_part) in enumerate(((cos_even, sin_even), (cos_odd, sin_odd))):
        columns_part(
            own.at[e], other.at[e], matrix, turned, turn_in, turn_out,
            cos_part, sin_part, 1, mixed.at[e],
        )

    def step(i, sums):
        rows = pl.ds(pl.multiple_of(i * BLOCK, BLOCK), BLOCK)
        real, imag = rows_back(mixed.at[0], mixed.at[1], turned, turn, rows)
        return product_part(real, imag, returned, phase_turn, product, rows, sums)

    zero = jnp.zeros((8, pixels), jnp.float32)
    sums = lax.fori_loop(0, pixels // BLOCK, step, (zero, zero, zero))
    weight_r, weight_i = weight_of(sums, pixels)
    weight_r, weight_i = weight_r * flag[0], weight_i * flag[0]

    def apply(i, carry):
        rows = pl.ds(pl.multiple_of(i * 32, 32), 32)
        pro_r, pro_i = product[0, rows, :], product[1, rows, :]
        out[0, rows, :] = weight_r * pro_r - weight_i * pro_i
        out[1, rows, :] = weight_r * pro_i + weight_i * pro_r
        return carry

    lax.fori_loop(0, pixels // 32, apply, 0)


def final_kernel(
    place, own, other, even, returned, phase_turn, drive,
    matrix, turned, turn, turn_in, turn_out, cos_part, sin_part, sent_r, sent_i, far_r, far_i, mixed, product, kept_r, kept_i, sems,
):
    pixels = returned.shape[1]
    columns_part(
        own, other, matrix, turned, turn_in, turn_out, cos_part, sin_part, 1, mixed
    )

    def step(i, sums):
        rows = pl.ds(pl.multiple_of(i * WIDE, WIDE), WIDE)
        real, imag = even_and_odd(even, mixed, turned, turn, rows)
        return product_part(real, imag, returned, phase_turn, product, rows, sums)

    zero = jnp.zeros((8, pixels), jnp.float32)
    sums = lax.fori_loop(0, pixels // WIDE, step, (zero, zero, zero))
    weight_r, weight_i = weight_of(sums, pixels)
    part = pixels // 4

    for out_r, out_i, core in ((kept_r, kept_i, place[0]), (sent_r, sent_i, 1 - place[0])):
        for s in range(2):

            def apply(i, carry, s=s, out_r=out_r, out_i=out_i, core=core):
                rows = pl.ds(pl.multiple_of((2 * s + core) * part + i * 32, 32), 32)
                to = pl.ds(pl.multiple_of(i * 32, 32), 32)
                pro_r, pro_i = product[0, rows, :], product[1, rows, :]
                out_r[s, to, :] = drive[0, rows, :] + (weight_r * pro_r - weight_i * pro_i)
                out_i[s, to, :] = drive[1, rows, :] + (weight_r * pro_i + weight_i * pro_r)
                return carry

            lax.fori_loop(0, part // 32, apply, 0)
        if out_r is kept_r:
            leaving = [
                pltpu.make_async_copy(kept_r, far_r, sems.at[0]),
                pltpu.make_async_copy(kept_i, far_i, sems.at[1]),
            ]
            for copy in leaving:
                copy.start()
    for copy in leaving:
        copy.wait()


def in_vmem(count):
    return [pl.BlockSpec(memory_space=pltpu.VMEM) for _ in range(count)]


def in_smem():
    return pl.BlockSpec(memory_space=pltpu.SMEM)


def limit(mebibytes):
    return pltpu.CompilerParams(vmem_limit_bytes=mebibytes * 1024 * 1024)


ROWS_LIMIT = 24
FIELD_LIMIT = 30
FINAL_LIMIT = 20


def far(value):
    return pltpu.with_memory_space_constraint(value, pltpu.HBM)


def rows_call(index, sources, plan, matrix, turn, bring=False):
    _, _, rows, pixels = sources[0].shape
    half = pixels // 2
    whole = jax.ShapeDtypeStruct((2, 2, rows, half), jnp.float32)
    part = jax.ShapeDtypeStruct((2, rows, half), jnp.float32)
    shapes = [shape for _, joined in plan for shape in ([whole] if joined else [part, part])]
    count = len(sources)

    def kernel(index, *refs):
        fields, refs = refs[:count], refs[count:]
        matrix, turn, refs = refs[0], refs[1], refs[2:]
        outs, scratch = list(refs[: len(shapes)]), refs[len(shapes) :]
        brought = []
        if bring:
            near_matrix, near_turn, table_sems = scratch[2:]
            brought = [
                pltpu.make_async_copy(turn, near_turn, table_sems.at[0]),
                pltpu.make_async_copy(matrix, near_matrix, table_sems.at[1]),
            ]
            matrix, turn = near_matrix, near_turn
        entries = []
        for at, (source, joined) in enumerate(plan):
            if joined:
                out = outs.pop(0)
                entries.append((fields[source], at, out.at[0], out.at[1]))
            else:
                entries.append((fields[source], at, outs.pop(0), outs.pop(0)))
        rows_kernel(entries, brought, index, matrix, turn, scratch[0], scratch[1])

    blocks = 2 * len(plan)
    scratch = [
        pltpu.VMEM((blocks, 2, rows // 2, pixels), jnp.float32),
        pltpu.SemaphoreType.DMA((blocks,)),
    ]
    table_specs = in_vmem(2)
    if bring:
        table_specs = [pl.BlockSpec(memory_space=pltpu.HBM)] * 2
        scratch += [
            pltpu.VMEM(matrix.shape, matrix.dtype),
            pltpu.VMEM(turn.shape, turn.dtype),
            pltpu.SemaphoreType.DMA((2,)),
        ]
        matrix, turn = far(matrix), far(turn)
    return pl.pallas_call(
        kernel,
        out_shape=tuple(shapes),
        in_specs=[in_smem()] + [pl.BlockSpec(memory_space=pltpu.HBM)] * count + table_specs,
        out_specs=tuple(in_vmem(len(shapes))),
        scratch_shapes=scratch,
        compiler_params=limit(ROWS_LIMIT),
        name="rows",
    )(index, *[far(source) for source in sources], matrix, turn)


def field_tables(tables):
    names = ("matrix", "turned", "turn", "turn_in", "turn_out", "cos_even", "sin_even", "cos_odd", "sin_odd")
    return [tables[name] for name in names]


def back_call(own, other, tables):
    half = own.shape[2]
    return pl.pallas_call(
        back_kernel,
        out_shape=jax.ShapeDtypeStruct((2, 2 * half, 2 * half), jnp.float32),
        in_specs=in_vmem(11),
        out_specs=in_vmem(1)[0],
        scratch_shapes=[pltpu.VMEM((2, 2, 2 * half, half), jnp.float32)],
        compiler_params=limit(FIELD_LIMIT),
        name="back",
    )(own, other, *field_tables(tables))


def even_call(own, other, tables):
    half = own.shape[1]
    return pl.pallas_call(
        even_kernel,
        out_shape=jax.ShapeDtypeStruct((2, 2 * half, half), jnp.float32),
        in_specs=in_vmem(8),
        out_specs=in_vmem(1)[0],
        scratch_shapes=[pltpu.VMEM((2, 2 * half, half), jnp.float32)],
        compiler_params=limit(FIELD_LIMIT),
        name="even",
    )(own, other, tables["matrix"], tables["turned"], tables["turn_in"],
      tables["turn_out"], tables["cos_even"], tables["sin_even"])


def last_call(flag, own, other, returned, phase_turn, tables):
    half = own.shape[2]
    return pl.pallas_call(
        last_kernel,
        out_shape=jax.ShapeDtypeStruct(returned.shape, jnp.float32),
        in_specs=[in_smem()] + in_vmem(13),
        out_specs=in_vmem(1)[0],
        scratch_shapes=[
            pltpu.VMEM((2, 2, 2 * half, half), jnp.float32),
            pltpu.VMEM(returned.shape, jnp.float32),
        ],
        compiler_params=limit(FIELD_LIMIT),
        name="last",
    )(flag.reshape(1), own, other, returned, phase_turn, *field_tables(tables))


def final_call(place, own, other, even, returned, phase_turn, drive, tables):
    pixels = returned.shape[1]
    part = jax.ShapeDtypeStruct((2, pixels // 4, pixels), jnp.float32)
    return pl.pallas_call(
        final_kernel,
        out_shape=(part,) * 2 + (pltpu.HBM(part.shape, part.dtype),) * 2,
        in_specs=[in_smem()] + in_vmem(13),
        out_specs=tuple(in_vmem(2)) + (pl.BlockSpec(memory_space=pltpu.HBM),) * 2,
        scratch_shapes=[
            pltpu.VMEM(even.shape, jnp.float32),
            pltpu.VMEM(returned.shape, jnp.float32),
            pltpu.VMEM(part.shape, part.dtype),
            pltpu.VMEM(part.shape, part.dtype),
            pltpu.SemaphoreType.DMA((2,)),
        ],
        compiler_params=limit(FINAL_LIMIT),
        name="final",
    )(place.reshape(1), own, other, even, returned, phase_turn, drive, tables["matrix"], tables["turned"],
      tables["turn"], tables["turn_in"], tables["turn_out"], tables["cos_odd"], tables["sin_odd"])


def circle(turns):
    quarters = 4.0 * turns
    nearest = jnp.round(quarters)
    angle = (quarters - nearest) * (0.5 * math.pi)
    square = angle * angle
    sin = 1.0 / 362880.0
    for term in (-1.0 / 5040.0, 1.0 / 120.0, -1.0 / 6.0, 1.0):
        sin = sin * square + term
    sin = sin * angle
    cos = -1.0 / 3628800.0
    for term in (1.0 / 40320.0, -1.0 / 720.0, 1.0 / 24.0, -0.5, 1.0):
        cos = cos * square + term
    count = nearest.astype(jnp.int32)
    swapped = (count & 1) == 1
    cos, sin = jnp.where(swapped, sin, cos), jnp.where(swapped, cos, sin)
    cos = jnp.where(((count + 1) & 2) == 2, -cos, cos)
    sin = jnp.where((count & 2) == 2, -sin, sin)
    return cos, sin


def turned_table(half):
    index = jnp.arange(half, dtype=jnp.int32)
    wrapped = index[:, None] * index[None, :] % half
    cos, sin = circle(wrapped.astype(jnp.float32) / half)
    value = jnp.concatenate(
        [jnp.concatenate([cos, sin], axis=1), jnp.concatenate([-sin, cos], axis=1)], axis=0
    )
    high = lax.reduce_precision(value, 8, 7)
    return jnp.stack([high.astype(jnp.bfloat16), (value - high).astype(jnp.bfloat16)])


def permuted_transfer(pixels, e):
    half = pixels // 2
    order = jnp.arange(2, dtype=jnp.int32)[:, None] + 2 * jnp.arange(half, dtype=jnp.int32)[None, :]
    signed = jnp.where(order < half, order, order - pixels).astype(jnp.float32)
    squared = signed[:, :, None] ** 2 + signed[e][None, None, :] ** 2
    scaled = squared * (wavelength / (pixels * pixel_pitch)) ** 2
    cos, sin = circle(-(gap_length / wavelength) * scaled / (1.0 + jnp.sqrt(1.0 - scaled)))
    return cos / (pixels * pixels), sin / (pixels * pixels)


def after(value, *others):
    return lax.optimization_barrier((value,) + others)[0]


def whole_modes(forward_fields, backward_fields, phase):
    pixels = forward_fields.shape[3]
    half = pixels // 2
    modes_here = forward_fields.shape[1]
    mode_size = lax.axis_size("mode")
    outer = mode_size // 4
    axes = ("mode", "space")
    mode_index = lax.axis_index("mode")
    space_index = lax.axis_index("space")
    core_index = mode_index % 2
    x_index = mode_index // 2 % 2
    z_index = mode_index // 4

    def flat(mode, space):
        return mode * 2 + space

    everyone = [(mode, space) for mode in range(mode_size) for space in range(2)]
    to_space = [(flat(m, s), flat(m, 1 - s)) for m, s in everyone]
    to_core = [(flat(m, s), flat(m ^ 1, s)) for m, s in everyone]
    to_x = [(flat(m, s), flat(m ^ 2, s)) for m, s in everyone]
    to_z = {j: [(flat(m, s), flat(m ^ (4 * j), s)) for m, s in everyone] for j in range(1, outer)}
    last_mode = [(flat(m, 1 - m % 2), flat(m, m % 2)) for m in range(mode_size)]

    def send(value, pairs):
        return lax.ppermute(value, axes, pairs)

    def swap_if(bit, value):
        return jnp.where(bit == 1, value[::-1], value)

    def by_z(value):
        shape = value.shape
        value = value.reshape((outer // 2, 2) + shape[1:])
        value = jnp.where(z_index % 2 == 1, value[:, ::-1], value)
        value = swap_if(z_index // 2, value)
        return value.reshape(shape)

    piece_rows = half // mode_size

    def share(value, bit, pairs):
        return swap_if(bit, jnp.stack([value, send(value, pairs)]))

    matrix = jnp.asarray(split_table(pixels))
    angle = 2.0 * np.pi / pixels * np.arange(half)
    turn = jnp.asarray(np.stack([np.cos(angle), np.sin(angle)]).astype(np.float32))

    last = jnp.full((), modes_here - 1, jnp.int32)
    both_fields = (backward_fields, forward_fields)
    (rows_last_backward,) = rows_call(
        last.reshape(1), (backward_fields,), ((0, True),), matrix, turn, True
    )
    got_last_backward = send(rows_last_backward, last_mode)
    quarter = half // 4
    part = lax.dynamic_slice_in_dim(
        phase, after(core_index * 2 + x_index, rows_last_backward) * quarter, quarter, axis=0
    )
    other_part = send(part, to_space)
    (rows_last_forward,) = rows_call(
        after(last, part).reshape(1), (forward_fields,), ((0, True),), matrix, turn
    )
    got_last_forward = send(rows_last_forward, last_mode)
    cos_even, sin_even = permuted_transfer(pixels, 0)
    cos_odd, sin_odd = permuted_transfer(pixels, 1)
    modes = jnp.stack([1 - space_index, 1 - space_index])
    sent_backward, sent_even, sent_odd = rows_call(
        after(modes, rows_last_forward), both_fields, ((0, True), (1, False)), matrix, turn
    )
    modes = jnp.stack([space_index, space_index])
    own_backward, own_even, own_odd = rows_call(
        after(modes, sent_odd), both_fields, ((0, True), (1, False)), matrix, turn
    )
    got_backward = send(sent_backward, to_space)
    got_even = send(sent_even, to_space)
    got_odd = send(sent_odd, to_space)

    other_part = after(other_part, own_odd)
    other_phase = share(share(other_part, x_index, to_x), core_index, to_core)
    whole_phase = swap_if(
        space_index, jnp.stack([phase, other_phase.reshape(half, pixels)])
    ).reshape(pixels, pixels)
    phase_turn = jnp.stack(circle(whole_phase * (0.5 / math.pi)))

    turn_out = jnp.broadcast_to(turn[:, :, None], (2, half, 128))
    tables = {
        "matrix": matrix,
        "turned": turned_table(half),
        "turn": turn,
        "turn_out": turn_out,
        "turn_in": turn_out * (1.0 - 2.0 * space_index.astype(jnp.float32)),
        "cos_even": cos_even,
        "sin_even": sin_even,
        "cos_odd": cos_odd,
        "sin_odd": sin_odd,
    }

    takes_last = jnp.where(space_index == core_index, 1.0, 0.0)
    returned = back_call(rows_last_backward, got_last_backward, tables)
    drive = last_call(
        takes_last, after(rows_last_forward, returned), got_last_forward, returned, phase_turn, tables
    )
    returned = back_call(after(own_backward, drive), got_backward, tables)
    even = even_call(after(own_even, returned), got_even, tables)
    sent_r, sent_i, kept_r, kept_i = final_call(
        core_index, own_odd, got_odd, even, returned, phase_turn, drive, tables
    )
    shape = (2, 2, outer, piece_rows, pixels)
    real = (kept_r + send(sent_r, to_core)).reshape(shape)
    imag = (kept_i + send(sent_i, to_core)).reshape(shape)

    def keep(value, axis, index):
        return lax.dynamic_index_in_dim(value, index, axis=axis, keepdims=False)

    def step(value, axis, index, pairs):
        return keep(value, axis, index) + send(keep(value, axis, 1 - index), pairs)

    real = step(real, 1, x_index, to_x)
    imag = step(imag, 0, space_index, to_space)
    real = step(real, 0, space_index, to_space)
    imag = step(imag, 0, x_index, to_x)
    both = by_z(jnp.stack([real, imag], axis=1))
    total = both[0]
    for j in range(1, outer):
        total = total + send(both[j], to_z[j])
    mode_root = math.sqrt(modes_here * mode_size)
    place = (core_index * 2 + x_index) * outer + z_index
    piece = lax.dynamic_slice_in_dim(phase, place * piece_rows, piece_rows, axis=0)
    updated = phase_update(total[0] / mode_root, total[1] / mode_root, piece)
    pieces = by_z(jnp.stack([updated] + [send(updated, to_z[j]) for j in range(1, outer)]))
    pieces = share(share(pieces, x_index, to_x), core_index, to_core)
    return pieces.reshape(half, pixels)


def on_device(forward_fields, backward_fields, phase):
    pixels = forward_fields.shape[3]
    if (
        lax.axis_size("space") == 2
        and lax.axis_size("mode") == 16
        and forward_fields.shape[1] == 3
        and pixels % 512 == 0
    ):
        return whole_modes(forward_fields, backward_fields, phase)
    return split_planes(forward_fields, backward_fields, phase)


def solution(mesh):
    in_specs = (P(None, "mode", "space", None), P(None, "mode", "space", None), P("space", None))
    out_specs = P("space", None)
    return jax.shard_map(
        on_device, mesh=mesh, in_specs=in_specs, out_specs=out_specs, check_vma=False
    )
```

```python
import math

import jax
import jax.numpy as jnp
import numpy as np
from jax import lax
from jax.experimental import pallas as pl
from jax.experimental.pallas import tpu as pltpu
from jax.sharding import PartitionSpec as P

gap_length = 0.02
wavelength = 1.55e-06
pixel_pitch = 8e-06
highest = lax.Precision.HIGHEST


def fourier_tables(pixels):
    indices = jnp.arange(pixels, dtype=jnp.int32)
    wrapped = indices[:, None] * indices[None, :] % pixels
    angles = 2.0 * math.pi / pixels * wrapped.astype(jnp.float32)
    return jnp.concatenate([jnp.cos(angles), jnp.sin(angles)], axis=1)


def transfer_block(pixels, first_column, col_width):
    indices = jnp.arange(pixels, dtype=jnp.int32)
    signed_rows = jnp.where(indices < pixels // 2, indices, indices - pixels).astype(jnp.float32)
    columns = first_column + jnp.arange(col_width, dtype=jnp.int32)
    signed_cols = jnp.where(columns < pixels // 2, columns, columns - pixels).astype(jnp.float32)
    squared = signed_rows[None, :] ** 2 + signed_cols[:, None] ** 2
    scaled = squared * (wavelength / (pixels * pixel_pitch)) ** 2
    angles = -2.0 * math.pi * (gap_length / wavelength) * scaled / (1.0 + jnp.sqrt(1.0 - scaled))
    return (jnp.cos(angles), jnp.sin(angles))


def rows_forward(fields, kernel, blocks):
    pixels = kernel.shape[0]
    rows_here = fields.shape[3]
    from_real = jnp.einsum("dkrx,xf->dkfr", fields[0], kernel, precision=highest)
    from_imag = jnp.einsum("dkrx,xf->dkfr", fields[1], kernel, precision=highest)
    spec_real = from_real[:, :, :pixels] + from_imag[:, :, pixels:]
    spec_imag = from_imag[:, :, :pixels] - from_real[:, :, pixels:]
    stacked = jnp.stack([spec_real, spec_imag])
    return stacked.reshape(
        2, fields.shape[1], fields.shape[2], blocks, pixels // blocks * rows_here
    )


def columns_section(column_data, kernel, cos_part, sin_part, directions, blocks):
    pixels = kernel.shape[0]
    rows_here = pixels // blocks
    col_width = column_data.shape[4] // rows_here
    depth = column_data.shape[1]
    items = column_data.shape[2]
    arranged = column_data.reshape(2, depth, items, blocks, col_width, rows_here)
    folded = kernel.reshape(blocks, rows_here, 2 * pixels)
    from_real = jnp.einsum("dkncr,nrf->dkcf", arranged[0], folded, precision=highest)
    from_imag = jnp.einsum("dkncr,nrf->dkcf", arranged[1], folded, precision=highest)
    freq_real = from_real[..., :pixels] + from_imag[..., pixels:]
    freq_imag = from_imag[..., :pixels] - from_real[..., pixels:]
    turned_sin = directions[:, None, None, None] * sin_part[None, None]
    moved_real = freq_real * cos_part - freq_imag * turned_sin
    moved_imag = freq_real * turned_sin + freq_imag * cos_part
    inverse_kernel = kernel.reshape(pixels, 2, blocks, rows_here)
    from_real = jnp.einsum("dkca,agnr->dkgncr", moved_real, inverse_kernel, precision=highest)
    from_imag = jnp.einsum("dkca,agnr->dkgncr", moved_imag, inverse_kernel, precision=highest)
    out_real = (from_real[:, :, 0] - from_imag[:, :, 1]) / pixels
    out_imag = (from_imag[:, :, 0] + from_real[:, :, 1]) / pixels
    stacked = jnp.stack([out_real, out_imag])
    return stacked.reshape(2, depth, items, blocks, col_width * rows_here)


def rows_inverse(column_data, kernel, blocks):
    pixels = kernel.shape[0]
    col_width = pixels // blocks
    rows_here = column_data.shape[4] // col_width
    arranged = column_data.reshape(
        2, column_data.shape[1], column_data.shape[2], blocks, col_width, rows_here
    )
    folded = kernel.reshape(blocks, col_width, 2 * pixels)
    from_real = jnp.einsum("dkncr,ncf->dkrf", arranged[0], folded, precision=highest)
    from_imag = jnp.einsum("dkncr,ncf->dkrf", arranged[1], folded, precision=highest)
    out_real = (from_real[..., :pixels] - from_imag[..., pixels:]) / pixels
    out_imag = (from_imag[..., :pixels] + from_real[..., pixels:]) / pixels
    return jnp.stack([out_real, out_imag])


def propagate(fields, directions, to_columns, to_rows, kernel, cos_part, sin_part, blocks):
    spectrum = rows_forward(fields, kernel, blocks)

    def column_work(column_data):
        return columns_section(column_data, kernel, cos_part, sin_part, directions, blocks)

    mixed = to_columns(spectrum, column_work)
    return rows_inverse(to_rows(mixed), kernel, blocks)


def phase_update(drive_real, drive_imag, phase):
    turned_imag = drive_real * jnp.sin(phase) + drive_imag * jnp.cos(phase)
    return phase - turned_imag / jnp.sqrt(drive_real * drive_real + drive_imag * drive_imag + 1.0)


def split_planes(forward_fields, backward_fields, phase):
    blocks = lax.axis_size("space")
    pixels = forward_fields.shape[3]
    per_device = forward_fields.shape[1]
    col_width = pixels // blocks
    kernel = fourier_tables(pixels)
    cos_part, sin_part = transfer_block(pixels, lax.axis_index("space") * col_width, col_width)
    arrived = propagate(
        forward_fields[:, None],
        jnp.ones((1,), jnp.float32),
        lambda payload, worker: worker(
            lax.all_to_all(payload, "space", split_axis=3, concat_axis=3, tiled=True)
        ),
        lambda payload: lax.all_to_all(payload, "space", split_axis=3, concat_axis=3, tiled=True),
        kernel,
        cos_part,
        sin_part,
        blocks,
    )[:, 0]
    returned = propagate(
        backward_fields[:, None],
        -jnp.ones((1,), jnp.float32),
        lambda payload, worker: worker(
            lax.all_to_all(payload, "space", split_axis=3, concat_axis=3, tiled=True)
        ),
        lambda payload: lax.all_to_all(payload, "space", split_axis=3, concat_axis=3, tiled=True),
        kernel,
        cos_part,
        sin_part,
        blocks,
    )[:, 0]
    product_real = returned[0] * arrived[0] + returned[1] * arrived[1]
    product_imag = returned[0] * arrived[1] - returned[1] * arrived[0]
    rotor_cos = jnp.cos(phase)
    rotor_sin = jnp.sin(phase)
    turn_real = product_real * rotor_cos - product_imag * rotor_sin
    turn_imag = product_real * rotor_sin + product_imag * rotor_cos
    local_real = jnp.sum(turn_real, axis=(1, 2)) / pixels
    local_imag = jnp.sum(turn_imag, axis=(1, 2)) / pixels
    local_power = jnp.sum(
        product_real * product_real + product_imag * product_imag, axis=(1, 2)
    ) / (pixels * pixels)
    correlation_real, correlation_imag, power_sum = lax.psum(
        (local_real, local_imag, local_power), "space"
    )
    inverse_norm = 1.0 / jnp.sqrt(
        correlation_real * correlation_real
        + correlation_imag * correlation_imag
        + power_sum
        + 1e-06
    )
    weight_real = (correlation_real * inverse_norm)[:, None, None]
    weight_imag = (-correlation_imag * inverse_norm)[:, None, None]
    drive_real = jnp.sum(weight_real * product_real - weight_imag * product_imag, axis=0)
    drive_imag = jnp.sum(weight_real * product_imag + weight_imag * product_real, axis=0)
    mode_root = math.sqrt(per_device * lax.axis_size("mode"))
    total_real, total_imag = lax.psum((drive_real, drive_imag), "mode")
    return phase_update(total_real / mode_root, total_imag / mode_root, phase)


def split_table(pixels):
    half = pixels // 2
    grid = np.outer(np.arange(half), np.arange(half)) % half
    angle = 2.0 * np.pi / half * grid
    cos, sin = np.cos(angle), np.sin(angle)
    matrix = np.block([[cos, -sin], [sin, cos]]).astype(np.float32)
    high = matrix.astype(jnp.bfloat16)
    low = (matrix - high.astype(np.float32)).astype(jnp.bfloat16)
    return np.stack([high, low])


def halves(value):
    high = value.astype(jnp.bfloat16)
    return high, (value - high.astype(jnp.float32)).astype(jnp.bfloat16)


def right_times(value, table):
    high, low = halves(value)
    left = jnp.concatenate([high, high, low], axis=1)
    right = jnp.concatenate([table[0], table[1], table[0]], axis=0)
    return jnp.dot(left, right, preferred_element_type=jnp.float32)


def left_times(table, value):
    high, low = halves(value)
    left = jnp.concatenate([table[0], table[1], table[0]], axis=1)
    right = jnp.concatenate([high, high, low], axis=0)
    return jnp.dot(left, right, preferred_element_type=jnp.float32)


def turn_back(real, imag, cos, sin):
    return real * cos + imag * sin, imag * cos - real * sin


def rows_kernel(plan, brought, index, matrix, turn, held, sems):
    rows = held.shape[2]
    blocks = plan[0][0].shape[2] // rows
    half = held.shape[3] // 2
    copies = [
        pltpu.make_async_copy(
            fields.at[:, index[at], pl.ds(i * rows, rows), :],
            held.at[n * blocks + i],
            sems.at[n * blocks + i],
        )
        for n, (fields, at, _, _) in enumerate(plan)
        for i in range(blocks)
    ]
    copies[0].start()
    for copy in brought:
        copy.start()
    for copy in copies[1:]:
        copy.start()
    for n, (_, _, even, odd) in enumerate(plan):
        for i in range(blocks):
            copies[n * blocks + i].wait()
            if n == 0 and i == 0:
                for copy in brought:
                    copy.wait()
            real, imag = held[n * blocks + i, 0], held[n * blocks + i, 1]
            sum_r, sum_i = real[:, :half] + real[:, half:], imag[:, :half] + imag[:, half:]
            odd_r, odd_i = turn_back(
                real[:, :half] - real[:, half:],
                imag[:, :half] - imag[:, half:],
                turn[0:1, :],
                turn[1:2, :],
            )
            stacked = jnp.concatenate(
                [
                    jnp.concatenate([sum_r, sum_i], axis=1),
                    jnp.concatenate([odd_r, odd_i], axis=1),
                ],
                axis=0,
            )
            result = right_times(stacked, matrix)
            to = pl.ds(i * rows, rows)
            even[0, to, :] = result[:rows, :half]
            even[1, to, :] = result[:rows, half:]
            odd[0, to, :] = result[rows:, :half]
            odd[1, to, :] = result[rows:, half:]


def columns_part(own, other, matrix, turned, turn_in, turn_out, cos_part, sin_part, sign, mixed):
    own_r, own_i = own[0], own[1]
    other_r, other_i = other[0], other[1]
    half, cols = own_r.shape

    def spread(value):
        return jnp.concatenate([value] * (cols // value.shape[1]), axis=1)

    odd_r, odd_i = turn_back(
        own_r - other_r, own_i - other_i, spread(turn_in[0]), spread(turn_in[1])
    )
    stacked = jnp.concatenate(
        [
            jnp.concatenate([own_r + other_r, odd_r], axis=1),
            jnp.concatenate([own_i + other_i, odd_i], axis=1),
        ],
        axis=0,
    )
    freq = left_times(turned, stacked)
    freq_r, freq_i = freq[:half], freq[half:]
    tc = jnp.concatenate([cos_part[0], cos_part[1]], axis=1)
    ts = jnp.concatenate([sin_part[0], sin_part[1]], axis=1)
    if isinstance(sign, int):
        ts = ts if sign > 0 else -ts
    else:
        ts = sign * ts
    moved_r, moved_i = freq_r * tc - freq_i * ts, freq_i * tc + freq_r * ts
    back = left_times(matrix, jnp.concatenate([moved_r, moved_i], axis=0))
    even_r, even_i = back[:half, :cols], back[half:, :cols]
    odd_r, odd_i = back[:half, cols:], back[half:, cols:]
    cos, sin = spread(turn_out[0]), spread(turn_out[1])
    add_r, add_i = odd_r * cos - odd_i * sin, odd_i * cos + odd_r * sin
    mixed[0, :half, :] = even_r + add_r
    mixed[1, :half, :] = even_i + add_i
    mixed[0, half:, :] = even_r - add_r
    mixed[1, half:, :] = even_i - add_i


def rows_back(mixed_even, mixed_odd, turned, turn, rows):
    stacked = jnp.concatenate(
        [
            jnp.concatenate([mixed_even[0, rows, :], mixed_even[1, rows, :]], axis=1),
            jnp.concatenate([mixed_odd[0, rows, :], mixed_odd[1, rows, :]], axis=1),
        ],
        axis=0,
    )
    back = right_times(stacked, turned)
    block = back.shape[0] // 2
    half = back.shape[1] // 2
    even_r, even_i = back[:block, :half], back[:block, half:]
    odd_r, odd_i = back[block:, :half], back[block:, half:]
    cos, sin = turn[0:1, :], turn[1:2, :]
    add_r, add_i = odd_r * cos - odd_i * sin, odd_i * cos + odd_r * sin
    return (
        jnp.concatenate([even_r + add_r, even_r - add_r], axis=1),
        jnp.concatenate([even_i + add_i, even_i - add_i], axis=1),
    )


BLOCK = 128
WIDE = 256


def add_sums(sums, pro_r, pro_i, cos, sin):
    def fold(value):
        return jnp.sum(value.reshape(value.shape[0] // 8, 8, value.shape[1]), axis=0)

    return (
        sums[0] + fold(pro_r * cos - pro_i * sin),
        sums[1] + fold(pro_r * sin + pro_i * cos),
        sums[2] + fold(pro_r * pro_r + pro_i * pro_i),
    )


def product_part(arr_r, arr_i, returned, phase_turn, product, rows, sums):
    ret_r, ret_i = returned[0, rows, :], returned[1, rows, :]
    pro_r, pro_i = ret_r * arr_r + ret_i * arr_i, ret_r * arr_i - ret_i * arr_r
    product[0, rows, :] = pro_r
    product[1, rows, :] = pro_i
    return add_sums(sums, pro_r, pro_i, phase_turn[0, rows, :], phase_turn[1, rows, :])


def back_kernel(
    own, other, matrix, turned, turn, turn_in, turn_out, cos_even, sin_even, cos_odd, sin_odd, out, mixed
):
    for e, (cos_part, sin_part) in enumerate(((cos_even, sin_even), (cos_odd, sin_odd))):
        columns_part(
            own.at[e], other.at[e], matrix, turned, turn_in, turn_out,
            cos_part, sin_part, -1, mixed.at[e],
        )

    def step(i, carry):
        rows = pl.ds(pl.multiple_of(i * BLOCK, BLOCK), BLOCK)
        real, imag = rows_back(mixed.at[0], mixed.at[1], turned, turn, rows)
        out[0, rows, :] = real
        out[1, rows, :] = imag
        return carry

    lax.fori_loop(0, out.shape[1] // BLOCK, step, 0)


def even_kernel(own, other, matrix, turned, turn_in, turn_out, cos_part, sin_part, out, mixed):
    columns_part(
        own, other, matrix, turned, turn_in, turn_out, cos_part, sin_part, 1, mixed
    )
    half = out.shape[2]
    for i in range(out.shape[1] // WIDE):
        rows = pl.ds(i * WIDE, WIDE)
        back = right_times(jnp.concatenate([mixed[0, rows, :], mixed[1, rows, :]], axis=1), turned)
        out[0, rows, :] = back[:, :half]
        out[1, rows, :] = back[:, half:]


def even_and_odd(even, mixed, turned, turn, rows):
    half = even.shape[2]
    back = right_times(jnp.concatenate([mixed[0, rows, :], mixed[1, rows, :]], axis=1), turned)
    odd_r, odd_i = back[:, :half], back[:, half:]
    cos, sin = turn[0:1, :], turn[1:2, :]
    add_r, add_i = odd_r * cos - odd_i * sin, odd_i * cos + odd_r * sin
    even_r, even_i = even[0, rows, :], even[1, rows, :]
    return (
        jnp.concatenate([even_r + add_r, even_r - add_r], axis=1),
        jnp.concatenate([even_i + add_i, even_i - add_i], axis=1),
    )


def shared_kernel(
    place, sign, own, other, matrix, turned, turn, turn_in, turn_out,
    cos_even, sin_even, cos_odd, sin_odd, sent, kept, mixed,
):
    half = own.shape[2]
    for e, (cos_part, sin_part) in enumerate(((cos_even, sin_even), (cos_odd, sin_odd))):
        columns_part(
            own.at[e], other.at[e], matrix, turned, turn_in, turn_out,
            cos_part, sin_part, sign[0], mixed.at[e],
        )
    for out, first in ((sent, (1 - place[0]) * half), (kept, place[0] * half)):

        def step(i, carry, out=out, first=first):
            rows = pl.ds(pl.multiple_of(first + i * BLOCK, BLOCK), BLOCK)
            to = pl.ds(pl.multiple_of(i * BLOCK, BLOCK), BLOCK)
            real, imag = rows_back(mixed.at[0], mixed.at[1], turned, turn, rows)
            out[0, to, :] = real
            out[1, to, :] = imag
            return carry

        lax.fori_loop(0, half // BLOCK, step, 0)


def totals(sums, pixels):
    def total(value):
        return jnp.sum(jnp.sum(value, axis=0, keepdims=True), axis=1, keepdims=True)

    return total(sums[0]) / pixels, total(sums[1]) / pixels, total(sums[2]) / (pixels * pixels)


def weight_of(cor_r, cor_i, power):
    norm = 1.0 / jnp.sqrt(cor_r * cor_r + cor_i * cor_i + power + 1e-06)
    return cor_r * norm, -cor_i * norm


def product_kernel(place, sign, mine, other, phase_turn, product, sums_out):
    half, pixels = mine.shape[1], mine.shape[2]
    block = 64

    def step(i, sums):
        rows = pl.ds(pl.multiple_of(i * block, block), block)
        at = pl.ds(pl.multiple_of(place[0] * half + i * block, block), block)
        turned_i = sign[0] * (other[0, rows, :] * mine[1, rows, :] - other[1, rows, :] * mine[0, rows, :])
        pro_r = other[0, rows, :] * mine[0, rows, :] + other[1, rows, :] * mine[1, rows, :]
        product[0, rows, :] = pro_r
        product[1, rows, :] = turned_i
        return add_sums(sums, pro_r, turned_i, phase_turn[0, at, :], phase_turn[1, at, :])

    zero = jnp.zeros((8, pixels), jnp.float32)
    sums = lax.fori_loop(0, half // block, step, (zero, zero, zero))
    for i, value in enumerate(totals(sums, pixels)):
        sums_out[i] = jnp.broadcast_to(value, sums_out.shape[1:])


def final_kernel(
    place, own, other, even, returned, phase_turn, shared, sums_here, sums_there,
    matrix, turned, turn, turn_in, turn_out, cos_part, sin_part, sent_r, sent_i, far_r, far_i, mixed, product, kept_r, kept_i, sems,
):
    pixels = returned.shape[1]
    columns_part(
        own, other, matrix, turned, turn_in, turn_out, cos_part, sin_part, 1, mixed
    )

    zero = jnp.zeros((8, pixels), jnp.float32)
    sums = (zero, zero, zero)
    for i in range(pixels // WIDE):
        rows = pl.ds(i * WIDE, WIDE)
        real, imag = even_and_odd(even, mixed, turned, turn, rows)
        sums = product_part(real, imag, returned, phase_turn, product, rows, sums)
    weight_r, weight_i = weight_of(*totals(sums, pixels))
    shared_r, shared_i = weight_of(
        *(sums_here[i, 0:1, 0:1] + sums_there[i, 0:1, 0:1] for i in range(3))
    )
    part = pixels // 4

    for out_r, out_i, core in ((kept_r, kept_i, place[0]), (sent_r, sent_i, 1 - place[0])):
        for s in range(2):

            here = jnp.where(place[0] == s, 1.0, 0.0)
            other_r, other_i = shared_r * here, shared_i * here

            def apply(i, carry, s=s, out_r=out_r, out_i=out_i, core=core, other_r=other_r, other_i=other_i):
                rows = pl.ds(pl.multiple_of((2 * s + core) * part + i * 32, 32), 32)
                at = pl.ds(pl.multiple_of(core * part + i * 32, 32), 32)
                to = pl.ds(pl.multiple_of(i * 32, 32), 32)
                pro_r, pro_i = product[0, rows, :], product[1, rows, :]
                sha_r, sha_i = shared[0, at, :], shared[1, at, :]
                out_r[s, to, :] = (weight_r * pro_r - weight_i * pro_i) + (
                    other_r * sha_r - other_i * sha_i
                )
                out_i[s, to, :] = (weight_r * pro_i + weight_i * pro_r) + (
                    other_r * sha_i + other_i * sha_r
                )
                return carry

            lax.fori_loop(0, part // 32, apply, 0)
        if out_r is kept_r:
            leaving = [
                pltpu.make_async_copy(kept_r, far_r, sems.at[0]),
                pltpu.make_async_copy(kept_i, far_i, sems.at[1]),
            ]
            for copy in leaving:
                copy.start()
    for copy in leaving:
        copy.wait()


def in_vmem(count):
    return [pl.BlockSpec(memory_space=pltpu.VMEM) for _ in range(count)]


def in_smem():
    return pl.BlockSpec(memory_space=pltpu.SMEM)


def limit(mebibytes):
    return pltpu.CompilerParams(vmem_limit_bytes=mebibytes * 1024 * 1024)


ROWS_LIMIT = 24
FIELD_LIMIT = 30
FINAL_LIMIT = 20


def far(value):
    return pltpu.with_memory_space_constraint(value, pltpu.HBM)


def rows_call(index, sources, plan, matrix, turn, bring=False):
    _, _, rows, pixels = sources[0].shape
    half = pixels // 2
    whole = jax.ShapeDtypeStruct((2, 2, rows, half), jnp.float32)
    part = jax.ShapeDtypeStruct((2, rows, half), jnp.float32)
    shapes = [shape for _, joined in plan for shape in ([whole] if joined else [part, part])]
    count = len(sources)

    def kernel(index, *refs):
        fields, refs = refs[:count], refs[count:]
        matrix, turn, refs = refs[0], refs[1], refs[2:]
        outs, scratch = list(refs[: len(shapes)]), refs[len(shapes) :]
        brought = []
        if bring:
            near_matrix, near_turn, table_sems = scratch[2:]
            brought = [
                pltpu.make_async_copy(turn, near_turn, table_sems.at[0]),
                pltpu.make_async_copy(matrix, near_matrix, table_sems.at[1]),
            ]
            matrix, turn = near_matrix, near_turn
        entries = []
        for at, (source, joined) in enumerate(plan):
            if joined:
                out = outs.pop(0)
                entries.append((fields[source], at, out.at[0], out.at[1]))
            else:
                entries.append((fields[source], at, outs.pop(0), outs.pop(0)))
        rows_kernel(entries, brought, index, matrix, turn, scratch[0], scratch[1])

    blocks = 2 * len(plan)
    scratch = [
        pltpu.VMEM((blocks, 2, rows // 2, pixels), jnp.float32),
        pltpu.SemaphoreType.DMA((blocks,)),
    ]
    table_specs = in_vmem(2)
    if bring:
        table_specs = [pl.BlockSpec(memory_space=pltpu.HBM)] * 2
        scratch += [
            pltpu.VMEM(matrix.shape, matrix.dtype),
            pltpu.VMEM(turn.shape, turn.dtype),
            pltpu.SemaphoreType.DMA((2,)),
        ]
        matrix, turn = far(matrix), far(turn)
    return pl.pallas_call(
        kernel,
        out_shape=tuple(shapes),
        in_specs=[in_smem()] + [pl.BlockSpec(memory_space=pltpu.HBM)] * count + table_specs,
        out_specs=tuple(in_vmem(len(shapes))),
        scratch_shapes=scratch,
        compiler_params=limit(ROWS_LIMIT),
        name="rows",
    )(index, *[far(source) for source in sources], matrix, turn)


def field_tables(tables):
    names = ("matrix", "turned", "turn", "turn_in", "turn_out", "cos_even", "sin_even", "cos_odd", "sin_odd")
    return [tables[name] for name in names]


def back_call(own, other, tables):
    half = own.shape[2]
    return pl.pallas_call(
        back_kernel,
        out_shape=jax.ShapeDtypeStruct((2, 2 * half, 2 * half), jnp.float32),
        in_specs=in_vmem(11),
        out_specs=in_vmem(1)[0],
        scratch_shapes=[pltpu.VMEM((2, 2, 2 * half, half), jnp.float32)],
        compiler_params=limit(FIELD_LIMIT),
        name="back",
    )(own, other, *field_tables(tables))


def even_call(own, other, tables):
    half = own.shape[1]
    return pl.pallas_call(
        even_kernel,
        out_shape=jax.ShapeDtypeStruct((2, 2 * half, half), jnp.float32),
        in_specs=in_vmem(8),
        out_specs=in_vmem(1)[0],
        scratch_shapes=[pltpu.VMEM((2, 2 * half, half), jnp.float32)],
        compiler_params=limit(FIELD_LIMIT),
        name="even",
    )(own, other, tables["matrix"], tables["turned"], tables["turn_in"],
      tables["turn_out"], tables["cos_even"], tables["sin_even"])


def shared_call(place, sign, own, other, tables):
    half = own.shape[2]
    part = jax.ShapeDtypeStruct((2, half, 2 * half), jnp.float32)
    return pl.pallas_call(
        shared_kernel,
        out_shape=(part, part),
        in_specs=[in_smem()] * 2 + in_vmem(11),
        out_specs=tuple(in_vmem(2)),
        scratch_shapes=[pltpu.VMEM((2, 2, 2 * half, half), jnp.float32)],
        compiler_params=limit(FIELD_LIMIT),
        name="shared",
    )(place.reshape(1), sign.reshape(1), own, other, *field_tables(tables))


def product_call(place, sign, mine, other, phase_turn):
    return pl.pallas_call(
        product_kernel,
        out_shape=(
            jax.ShapeDtypeStruct(mine.shape, jnp.float32),
            jax.ShapeDtypeStruct((3, 8, 128), jnp.float32),
        ),
        in_specs=[in_smem()] * 2 + in_vmem(3),
        out_specs=tuple(in_vmem(2)),
        compiler_params=limit(ROWS_LIMIT),
        name="product",
    )(place.reshape(1), sign.reshape(1), mine, other, phase_turn)


def final_call(place, own, other, even, returned, phase_turn, shared, sums_here, sums_there, tables):
    pixels = returned.shape[1]
    part = jax.ShapeDtypeStruct((2, pixels // 4, pixels), jnp.float32)
    return pl.pallas_call(
        final_kernel,
        out_shape=(part,) * 2 + (pltpu.HBM(part.shape, part.dtype),) * 2,
        in_specs=[in_smem()] + in_vmem(15),
        out_specs=tuple(in_vmem(2)) + (pl.BlockSpec(memory_space=pltpu.HBM),) * 2,
        scratch_shapes=[
            pltpu.VMEM(even.shape, jnp.float32),
            pltpu.VMEM(returned.shape, jnp.float32),
            pltpu.VMEM(part.shape, part.dtype),
            pltpu.VMEM(part.shape, part.dtype),
            pltpu.SemaphoreType.DMA((2,)),
        ],
        compiler_params=limit(FINAL_LIMIT),
        name="final",
    )(place.reshape(1), own, other, even, returned, phase_turn, shared, sums_here, sums_there, tables["matrix"], tables["turned"],
      tables["turn"], tables["turn_in"], tables["turn_out"], tables["cos_odd"], tables["sin_odd"])


def circle(turns):
    quarters = 4.0 * turns
    nearest = jnp.round(quarters)
    angle = (quarters - nearest) * (0.5 * math.pi)
    square = angle * angle
    sin = 1.0 / 362880.0
    for term in (-1.0 / 5040.0, 1.0 / 120.0, -1.0 / 6.0, 1.0):
        sin = sin * square + term
    sin = sin * angle
    cos = -1.0 / 3628800.0
    for term in (1.0 / 40320.0, -1.0 / 720.0, 1.0 / 24.0, -0.5, 1.0):
        cos = cos * square + term
    count = nearest.astype(jnp.int32)
    swapped = (count & 1) == 1
    cos, sin = jnp.where(swapped, sin, cos), jnp.where(swapped, cos, sin)
    cos = jnp.where(((count + 1) & 2) == 2, -cos, cos)
    sin = jnp.where((count & 2) == 2, -sin, sin)
    return cos, sin


def turned_table(half):
    index = jnp.arange(half, dtype=jnp.int32)
    wrapped = index[:, None] * index[None, :] % half
    cos, sin = circle(wrapped.astype(jnp.float32) / half)
    value = jnp.concatenate(
        [jnp.concatenate([cos, sin], axis=1), jnp.concatenate([-sin, cos], axis=1)], axis=0
    )
    high = lax.reduce_precision(value, 8, 7)
    return jnp.stack([high.astype(jnp.bfloat16), (value - high).astype(jnp.bfloat16)])


def permuted_transfer(pixels, e):
    half = pixels // 2
    order = jnp.arange(2, dtype=jnp.int32)[:, None] + 2 * jnp.arange(half, dtype=jnp.int32)[None, :]
    signed = jnp.where(order < half, order, order - pixels).astype(jnp.float32)
    squared = signed[:, :, None] ** 2 + signed[e][None, None, :] ** 2
    scaled = squared * (wavelength / (pixels * pixel_pitch)) ** 2
    cos, sin = circle(-(gap_length / wavelength) * scaled / (1.0 + jnp.sqrt(1.0 - scaled)))
    return cos / (pixels * pixels), sin / (pixels * pixels)


def after(value, *others):
    return lax.optimization_barrier((value,) + others)[0]


def whole_modes(forward_fields, backward_fields, phase):
    pixels = forward_fields.shape[3]
    half = pixels // 2
    modes_here = forward_fields.shape[1]
    mode_size = lax.axis_size("mode")
    outer = mode_size // 4
    axes = ("mode", "space")
    mode_index = lax.axis_index("mode")
    space_index = lax.axis_index("space")
    core_index = mode_index % 2
    x_index = mode_index // 2 % 2
    z_index = mode_index // 4

    def flat(mode, space):
        return mode * 2 + space

    everyone = [(mode, space) for mode in range(mode_size) for space in range(2)]
    to_space = [(flat(m, s), flat(m, 1 - s)) for m, s in everyone]
    to_core = [(flat(m, s), flat(m ^ 1, s)) for m, s in everyone]
    to_x = [(flat(m, s), flat(m ^ 2, s)) for m, s in everyone]
    to_z = {j: [(flat(m, s), flat(m ^ (4 * j), s)) for m, s in everyone] for j in range(1, outer)}

    def send(value, pairs):
        return lax.ppermute(value, axes, pairs)

    def swap_if(bit, value):
        return jnp.where(bit == 1, value[::-1], value)

    def by_z(value):
        shape = value.shape
        value = value.reshape((outer // 2, 2) + shape[1:])
        value = jnp.where(z_index % 2 == 1, value[:, ::-1], value)
        value = swap_if(z_index // 2, value)
        return value.reshape(shape)

    piece_rows = half // mode_size

    def share(value, bit, pairs):
        return swap_if(bit, jnp.stack([value, send(value, pairs)]))

    matrix = jnp.asarray(split_table(pixels))
    angle = 2.0 * np.pi / pixels * np.arange(half)
    turn = jnp.asarray(np.stack([np.cos(angle), np.sin(angle)]).astype(np.float32))

    last = jnp.full((), modes_here - 1, jnp.int32)
    both_fields = (backward_fields, forward_fields)
    (sent_backward,) = rows_call(
        (1 - space_index).reshape(1), (backward_fields,), ((0, True),), matrix, turn, True
    )
    got_backward = send(sent_backward, to_space)
    quarter = half // 4
    part = lax.dynamic_slice_in_dim(
        phase, after(core_index * 2 + x_index, sent_backward) * quarter, quarter, axis=0
    )
    other_part = send(part, to_space)
    last_backward, last_forward = rows_call(
        after(jnp.stack([last, last]), part), both_fields, ((0, True), (1, True)), matrix, turn
    )
    core_backward = send(last_backward, to_core)
    modes = jnp.stack([1 - space_index])
    sent_even, sent_odd = rows_call(
        after(modes, last_backward), (forward_fields,), ((0, False),), matrix, turn
    )
    stays = core_index == space_index
    sent_shared = jnp.where(stays, core_backward, last_forward)
    got_shared = send(sent_shared, to_space)
    own_shared = jnp.where(stays, last_forward, core_backward)
    got_even = send(sent_even, to_space)
    got_odd = send(sent_odd, to_space)
    cos_even, sin_even = permuted_transfer(pixels, 0)
    cos_odd, sin_odd = permuted_transfer(pixels, 1)
    modes = jnp.stack([space_index, space_index])
    own_backward, own_even, own_odd = rows_call(
        after(modes, sent_odd, sent_shared), both_fields, ((0, True), (1, False)), matrix, turn
    )

    other_part = after(other_part, own_odd)
    other_phase = share(share(other_part, x_index, to_x), core_index, to_core)
    whole_phase = swap_if(
        space_index, jnp.stack([phase, other_phase.reshape(half, pixels)])
    ).reshape(pixels, pixels)
    phase_turn = jnp.stack(circle(whole_phase * (0.5 / math.pi)))

    turn_out = jnp.broadcast_to(turn[:, :, None], (2, half, 128))
    tables = {
        "matrix": matrix,
        "turned": turned_table(half),
        "turn": turn,
        "turn_out": turn_out,
        "turn_in": turn_out * (1.0 - 2.0 * space_index.astype(jnp.float32)),
        "cos_even": cos_even,
        "sin_even": sin_even,
        "cos_odd": cos_odd,
        "sin_odd": sin_odd,
    }

    sign = jnp.where(stays, 1.0, -1.0)
    returned = back_call(own_backward, got_backward, tables)
    give, mine = shared_call(core_index, sign, after(own_shared, returned), got_shared, tables)
    shared, sums_here = product_call(core_index, sign, mine, send(give, to_core), phase_turn)
    sums_there = send(sums_here, to_core)
    even = even_call(after(own_even, sums_here), got_even, tables)
    sent_r, sent_i, kept_r, kept_i = final_call(
        core_index, own_odd, got_odd, even, returned, phase_turn, shared, sums_here, sums_there, tables
    )
    shape = (2, 2, outer, piece_rows, pixels)

    def keep(value, axis, index):
        return lax.dynamic_index_in_dim(value, index, axis=axis, keepdims=False)

    def core_step(kept, sent, axis, index, pairs):
        kept, got = kept.reshape(shape), send(sent, to_core).reshape(shape)
        leaves = keep(kept, axis, 1 - index) + keep(got, axis, 1 - index)
        return keep(kept, axis, index) + keep(got, axis, index) + send(leaves, pairs)

    def step(value, axis, index, pairs):
        return keep(value, axis, index) + send(keep(value, axis, 1 - index), pairs)

    real = core_step(kept_r, sent_r, 1, x_index, to_x)
    imag = core_step(kept_i, sent_i, 0, space_index, to_space)
    real = step(real, 0, space_index, to_space)
    imag = step(imag, 0, x_index, to_x)
    both = by_z(jnp.stack([real, imag], axis=1))
    got = {j: send(both[j], to_z[j]) for j in range(1, outer)}
    total = both[0]
    for j in range(1, outer):
        total = total + got[j]
    mode_root = math.sqrt(modes_here * mode_size)
    place = (core_index * 2 + x_index) * outer + z_index
    piece = lax.dynamic_slice_in_dim(phase, place * piece_rows, piece_rows, axis=0)
    updated = phase_update(total[0] / mode_root, total[1] / mode_root, piece)
    got = {j: send(updated, to_z[j]) for j in range(1, outer)}
    pieces = by_z(jnp.stack([updated] + [got[j] for j in range(1, outer)]))
    pieces = share(share(pieces, x_index, to_x), core_index, to_core)
    return pieces.reshape(half, pixels)


def on_device(forward_fields, backward_fields, phase):
    pixels = forward_fields.shape[3]
    if (
        lax.axis_size("space") == 2
        and lax.axis_size("mode") == 16
        and forward_fields.shape[1] == 3
        and pixels % 512 == 0
    ):
        return whole_modes(forward_fields, backward_fields, phase)
    return split_planes(forward_fields, backward_fields, phase)


def solution(mesh):
    in_specs = (P(None, "mode", "space", None), P(None, "mode", "space", None), P("space", None))
    out_specs = P("space", None)
    return jax.shard_map(
        on_device, mesh=mesh, in_specs=in_specs, out_specs=out_specs, check_vma=False
    )
```

```python
import math

import jax
import jax.numpy as jnp
import numpy as np
from jax import lax
from jax.experimental import pallas as pl
from jax.experimental.pallas import tpu as pltpu
from jax.sharding import PartitionSpec as P

gap_length = 0.02
wavelength = 1.55e-06
pixel_pitch = 8e-06
highest = lax.Precision.HIGHEST


def fourier_tables(pixels):
    indices = jnp.arange(pixels, dtype=jnp.int32)
    wrapped = indices[:, None] * indices[None, :] % pixels
    angles = 2.0 * math.pi / pixels * wrapped.astype(jnp.float32)
    return jnp.concatenate([jnp.cos(angles), jnp.sin(angles)], axis=1)


def transfer_block(pixels, first_column, col_width):
    indices = jnp.arange(pixels, dtype=jnp.int32)
    signed_rows = jnp.where(indices < pixels // 2, indices, indices - pixels).astype(jnp.float32)
    columns = first_column + jnp.arange(col_width, dtype=jnp.int32)
    signed_cols = jnp.where(columns < pixels // 2, columns, columns - pixels).astype(jnp.float32)
    squared = signed_rows[None, :] ** 2 + signed_cols[:, None] ** 2
    scaled = squared * (wavelength / (pixels * pixel_pitch)) ** 2
    angles = -2.0 * math.pi * (gap_length / wavelength) * scaled / (1.0 + jnp.sqrt(1.0 - scaled))
    return (jnp.cos(angles), jnp.sin(angles))


def rows_forward(fields, kernel, blocks):
    pixels = kernel.shape[0]
    rows_here = fields.shape[3]
    from_real = jnp.einsum("dkrx,xf->dkfr", fields[0], kernel, precision=highest)
    from_imag = jnp.einsum("dkrx,xf->dkfr", fields[1], kernel, precision=highest)
    spec_real = from_real[:, :, :pixels] + from_imag[:, :, pixels:]
    spec_imag = from_imag[:, :, :pixels] - from_real[:, :, pixels:]
    stacked = jnp.stack([spec_real, spec_imag])
    return stacked.reshape(
        2, fields.shape[1], fields.shape[2], blocks, pixels // blocks * rows_here
    )


def columns_section(column_data, kernel, cos_part, sin_part, directions, blocks):
    pixels = kernel.shape[0]
    rows_here = pixels // blocks
    col_width = column_data.shape[4] // rows_here
    depth = column_data.shape[1]
    items = column_data.shape[2]
    arranged = column_data.reshape(2, depth, items, blocks, col_width, rows_here)
    folded = kernel.reshape(blocks, rows_here, 2 * pixels)
    from_real = jnp.einsum("dkncr,nrf->dkcf", arranged[0], folded, precision=highest)
    from_imag = jnp.einsum("dkncr,nrf->dkcf", arranged[1], folded, precision=highest)
    freq_real = from_real[..., :pixels] + from_imag[..., pixels:]
    freq_imag = from_imag[..., :pixels] - from_real[..., pixels:]
    turned_sin = directions[:, None, None, None] * sin_part[None, None]
    moved_real = freq_real * cos_part - freq_imag * turned_sin
    moved_imag = freq_real * turned_sin + freq_imag * cos_part
    inverse_kernel = kernel.reshape(pixels, 2, blocks, rows_here)
    from_real = jnp.einsum("dkca,agnr->dkgncr", moved_real, inverse_kernel, precision=highest)
    from_imag = jnp.einsum("dkca,agnr->dkgncr", moved_imag, inverse_kernel, precision=highest)
    out_real = (from_real[:, :, 0] - from_imag[:, :, 1]) / pixels
    out_imag = (from_imag[:, :, 0] + from_real[:, :, 1]) / pixels
    stacked = jnp.stack([out_real, out_imag])
    return stacked.reshape(2, depth, items, blocks, col_width * rows_here)


def rows_inverse(column_data, kernel, blocks):
    pixels = kernel.shape[0]
    col_width = pixels // blocks
    rows_here = column_data.shape[4] // col_width
    arranged = column_data.reshape(
        2, column_data.shape[1], column_data.shape[2], blocks, col_width, rows_here
    )
    folded = kernel.reshape(blocks, col_width, 2 * pixels)
    from_real = jnp.einsum("dkncr,ncf->dkrf", arranged[0], folded, precision=highest)
    from_imag = jnp.einsum("dkncr,ncf->dkrf", arranged[1], folded, precision=highest)
    out_real = (from_real[..., :pixels] - from_imag[..., pixels:]) / pixels
    out_imag = (from_imag[..., :pixels] + from_real[..., pixels:]) / pixels
    return jnp.stack([out_real, out_imag])


def propagate(fields, directions, to_columns, to_rows, kernel, cos_part, sin_part, blocks):
    spectrum = rows_forward(fields, kernel, blocks)

    def column_work(column_data):
        return columns_section(column_data, kernel, cos_part, sin_part, directions, blocks)

    mixed = to_columns(spectrum, column_work)
    return rows_inverse(to_rows(mixed), kernel, blocks)


def phase_update(drive_real, drive_imag, phase):
    turned_imag = drive_real * jnp.sin(phase) + drive_imag * jnp.cos(phase)
    return phase - turned_imag / jnp.sqrt(drive_real * drive_real + drive_imag * drive_imag + 1.0)


def split_planes(forward_fields, backward_fields, phase):
    blocks = lax.axis_size("space")
    pixels = forward_fields.shape[3]
    per_device = forward_fields.shape[1]
    col_width = pixels // blocks
    kernel = fourier_tables(pixels)
    cos_part, sin_part = transfer_block(pixels, lax.axis_index("space") * col_width, col_width)
    arrived = propagate(
        forward_fields[:, None],
        jnp.ones((1,), jnp.float32),
        lambda payload, worker: worker(
            lax.all_to_all(payload, "space", split_axis=3, concat_axis=3, tiled=True)
        ),
        lambda payload: lax.all_to_all(payload, "space", split_axis=3, concat_axis=3, tiled=True),
        kernel,
        cos_part,
        sin_part,
        blocks,
    )[:, 0]
    returned = propagate(
        backward_fields[:, None],
        -jnp.ones((1,), jnp.float32),
        lambda payload, worker: worker(
            lax.all_to_all(payload, "space", split_axis=3, concat_axis=3, tiled=True)
        ),
        lambda payload: lax.all_to_all(payload, "space", split_axis=3, concat_axis=3, tiled=True),
        kernel,
        cos_part,
        sin_part,
        blocks,
    )[:, 0]
    product_real = returned[0] * arrived[0] + returned[1] * arrived[1]
    product_imag = returned[0] * arrived[1] - returned[1] * arrived[0]
    rotor_cos = jnp.cos(phase)
    rotor_sin = jnp.sin(phase)
    turn_real = product_real * rotor_cos - product_imag * rotor_sin
    turn_imag = product_real * rotor_sin + product_imag * rotor_cos
    local_real = jnp.sum(turn_real, axis=(1, 2)) / pixels
    local_imag = jnp.sum(turn_imag, axis=(1, 2)) / pixels
    local_power = jnp.sum(
        product_real * product_real + product_imag * product_imag, axis=(1, 2)
    ) / (pixels * pixels)
    correlation_real, correlation_imag, power_sum = lax.psum(
        (local_real, local_imag, local_power), "space"
    )
    inverse_norm = 1.0 / jnp.sqrt(
        correlation_real * correlation_real
        + correlation_imag * correlation_imag
        + power_sum
        + 1e-06
    )
    weight_real = (correlation_real * inverse_norm)[:, None, None]
    weight_imag = (-correlation_imag * inverse_norm)[:, None, None]
    drive_real = jnp.sum(weight_real * product_real - weight_imag * product_imag, axis=0)
    drive_imag = jnp.sum(weight_real * product_imag + weight_imag * product_real, axis=0)
    mode_root = math.sqrt(per_device * lax.axis_size("mode"))
    total_real, total_imag = lax.psum((drive_real, drive_imag), "mode")
    return phase_update(total_real / mode_root, total_imag / mode_root, phase)


def split_table(pixels):
    half = pixels // 2
    grid = np.outer(np.arange(half), np.arange(half)) % half
    angle = 2.0 * np.pi / half * grid
    cos, sin = np.cos(angle), np.sin(angle)
    matrix = np.block([[cos, -sin], [sin, cos]]).astype(np.float32)
    high = matrix.astype(jnp.bfloat16)
    low = (matrix - high.astype(np.float32)).astype(jnp.bfloat16)
    return np.stack([high, low])


def halves(value):
    high = value.astype(jnp.bfloat16)
    return high, (value - high.astype(jnp.float32)).astype(jnp.bfloat16)


def right_times(value, table):
    high, low = halves(value)
    left = jnp.concatenate([high, high, low], axis=1)
    right = jnp.concatenate([table[0], table[1], table[0]], axis=0)
    return jnp.dot(left, right, preferred_element_type=jnp.float32)


def left_times(table, value):
    high, low = halves(value)
    left = jnp.concatenate([table[0], table[1], table[0]], axis=1)
    right = jnp.concatenate([high, high, low], axis=0)
    return jnp.dot(left, right, preferred_element_type=jnp.float32)


def turn_back(real, imag, cos, sin):
    return real * cos + imag * sin, imag * cos - real * sin


def rows_kernel(plan, brought, index, matrix, turn, held, sems):
    rows = held.shape[2]
    blocks = plan[0][0].shape[2] // rows
    half = held.shape[3] // 2
    copies = [
        pltpu.make_async_copy(
            fields.at[:, index[at], pl.ds(i * rows, rows), :],
            held.at[n * blocks + i],
            sems.at[n * blocks + i],
        )
        for n, (fields, at, _, _) in enumerate(plan)
        for i in range(blocks)
    ]
    copies[0].start()
    for copy in brought:
        copy.start()
    for copy in copies[1:]:
        copy.start()
    for n, (_, _, even, odd) in enumerate(plan):
        for i in range(blocks):
            copies[n * blocks + i].wait()
            if n == 0 and i == 0:
                for copy in brought:
                    copy.wait()
            real, imag = held[n * blocks + i, 0], held[n * blocks + i, 1]
            sum_r, sum_i = real[:, :half] + real[:, half:], imag[:, :half] + imag[:, half:]
            odd_r, odd_i = turn_back(
                real[:, :half] - real[:, half:],
                imag[:, :half] - imag[:, half:],
                turn[0:1, :],
                turn[1:2, :],
            )
            stacked = jnp.concatenate(
                [
                    jnp.concatenate([sum_r, sum_i], axis=1),
                    jnp.concatenate([odd_r, odd_i], axis=1),
                ],
                axis=0,
            )
            result = right_times(stacked, matrix)
            to = pl.ds(i * rows, rows)
            even[0, to, :] = result[:rows, :half]
            even[1, to, :] = result[:rows, half:]
            odd[0, to, :] = result[rows:, :half]
            odd[1, to, :] = result[rows:, half:]


def columns_part(own, other, matrix, turned, turn_in, turn_out, cos_part, sin_part, sign, mixed):
    own_r, own_i = own[0], own[1]
    other_r, other_i = other[0], other[1]
    half, cols = own_r.shape

    def spread(value):
        return jnp.concatenate([value] * (cols // value.shape[1]), axis=1)

    odd_r, odd_i = turn_back(
        own_r - other_r, own_i - other_i, spread(turn_in[0]), spread(turn_in[1])
    )
    stacked = jnp.concatenate(
        [
            jnp.concatenate([own_r + other_r, odd_r], axis=1),
            jnp.concatenate([own_i + other_i, odd_i], axis=1),
        ],
        axis=0,
    )
    freq = left_times(turned, stacked)
    freq_r, freq_i = freq[:half], freq[half:]
    tc = jnp.concatenate([cos_part[0], cos_part[1]], axis=1)
    ts = jnp.concatenate([sin_part[0], sin_part[1]], axis=1)
    if isinstance(sign, int):
        ts = ts if sign > 0 else -ts
    else:
        ts = sign * ts
    moved_r, moved_i = freq_r * tc - freq_i * ts, freq_i * tc + freq_r * ts
    back = left_times(matrix, jnp.concatenate([moved_r, moved_i], axis=0))
    even_r, even_i = back[:half, :cols], back[half:, :cols]
    odd_r, odd_i = back[:half, cols:], back[half:, cols:]
    cos, sin = spread(turn_out[0]), spread(turn_out[1])
    add_r, add_i = odd_r * cos - odd_i * sin, odd_i * cos + odd_r * sin
    mixed[0, :half, :] = even_r + add_r
    mixed[1, :half, :] = even_i + add_i
    mixed[0, half:, :] = even_r - add_r
    mixed[1, half:, :] = even_i - add_i


def rows_back(mixed_even, mixed_odd, turned, turn, rows):
    stacked = jnp.concatenate(
        [
            jnp.concatenate([mixed_even[0, rows, :], mixed_even[1, rows, :]], axis=1),
            jnp.concatenate([mixed_odd[0, rows, :], mixed_odd[1, rows, :]], axis=1),
        ],
        axis=0,
    )
    back = right_times(stacked, turned)
    block = back.shape[0] // 2
    half = back.shape[1] // 2
    even_r, even_i = back[:block, :half], back[:block, half:]
    odd_r, odd_i = back[block:, :half], back[block:, half:]
    cos, sin = turn[0:1, :], turn[1:2, :]
    add_r, add_i = odd_r * cos - odd_i * sin, odd_i * cos + odd_r * sin
    return (
        jnp.concatenate([even_r + add_r, even_r - add_r], axis=1),
        jnp.concatenate([even_i + add_i, even_i - add_i], axis=1),
    )


BLOCK = 128
WIDE = 256


def add_sums(sums, pro_r, pro_i, cos, sin):
    def fold(value):
        return jnp.sum(value.reshape(value.shape[0] // 8, 8, value.shape[1]), axis=0)

    return (
        sums[0] + fold(pro_r * cos - pro_i * sin),
        sums[1] + fold(pro_r * sin + pro_i * cos),
        sums[2] + fold(pro_r * pro_r + pro_i * pro_i),
    )


def product_part(arr_r, arr_i, returned, phase_turn, product, rows, sums):
    ret_r, ret_i = returned[0, rows, :], returned[1, rows, :]
    pro_r, pro_i = ret_r * arr_r + ret_i * arr_i, ret_r * arr_i - ret_i * arr_r
    product[0, rows, :] = pro_r
    product[1, rows, :] = pro_i
    return add_sums(sums, pro_r, pro_i, phase_turn[0, rows, :], phase_turn[1, rows, :])


def back_kernel(
    own, other, matrix, turned, turn, turn_in, turn_out, cos_even, sin_even, cos_odd, sin_odd, out, mixed
):
    for e, (cos_part, sin_part) in enumerate(((cos_even, sin_even), (cos_odd, sin_odd))):
        columns_part(
            own.at[e], other.at[e], matrix, turned, turn_in, turn_out,
            cos_part, sin_part, -1, mixed.at[e],
        )

    def step(i, carry):
        rows = pl.ds(pl.multiple_of(i * BLOCK, BLOCK), BLOCK)
        real, imag = rows_back(mixed.at[0], mixed.at[1], turned, turn, rows)
        out[0, rows, :] = real
        out[1, rows, :] = imag
        return carry

    lax.fori_loop(0, out.shape[1] // BLOCK, step, 0)


def even_kernel(own, other, matrix, turned, turn_in, turn_out, cos_part, sin_part, out, mixed):
    columns_part(
        own, other, matrix, turned, turn_in, turn_out, cos_part, sin_part, 1, mixed
    )
    half = out.shape[2]
    for i in range(out.shape[1] // WIDE):
        rows = pl.ds(i * WIDE, WIDE)
        back = right_times(jnp.concatenate([mixed[0, rows, :], mixed[1, rows, :]], axis=1), turned)
        out[0, rows, :] = back[:, :half]
        out[1, rows, :] = back[:, half:]


def even_and_odd(even, mixed, turned, turn, rows):
    half = even.shape[2]
    back = right_times(jnp.concatenate([mixed[0, rows, :], mixed[1, rows, :]], axis=1), turned)
    odd_r, odd_i = back[:, :half], back[:, half:]
    cos, sin = turn[0:1, :], turn[1:2, :]
    add_r, add_i = odd_r * cos - odd_i * sin, odd_i * cos + odd_r * sin
    even_r, even_i = even[0, rows, :], even[1, rows, :]
    return (
        jnp.concatenate([even_r + add_r, even_r - add_r], axis=1),
        jnp.concatenate([even_i + add_i, even_i - add_i], axis=1),
    )


def shared_kernel(
    place, sign, own, other, matrix, turned, turn, turn_in, turn_out,
    cos_even, sin_even, cos_odd, sin_odd, sent, kept, mixed,
):
    half = own.shape[2]
    for e, (cos_part, sin_part) in enumerate(((cos_even, sin_even), (cos_odd, sin_odd))):
        columns_part(
            own.at[e], other.at[e], matrix, turned, turn_in, turn_out,
            cos_part, sin_part, sign[0], mixed.at[e],
        )
    for out, first in ((sent, (1 - place[0]) * half), (kept, place[0] * half)):

        def step(i, carry, out=out, first=first):
            rows = pl.ds(pl.multiple_of(first + i * BLOCK, BLOCK), BLOCK)
            to = pl.ds(pl.multiple_of(i * BLOCK, BLOCK), BLOCK)
            real, imag = rows_back(mixed.at[0], mixed.at[1], turned, turn, rows)
            out[0, to, :] = real
            out[1, to, :] = imag
            return carry

        lax.fori_loop(0, half // BLOCK, step, 0)


def totals(sums, pixels):
    def total(value):
        return jnp.sum(jnp.sum(value, axis=0, keepdims=True), axis=1, keepdims=True)

    return total(sums[0]) / pixels, total(sums[1]) / pixels, total(sums[2]) / (pixels * pixels)


def weight_of(cor_r, cor_i, power):
    norm = 1.0 / jnp.sqrt(cor_r * cor_r + cor_i * cor_i + power + 1e-06)
    return cor_r * norm, -cor_i * norm


def product_kernel(place, sign, mine, other, phase_turn, product, sums_out):
    half, pixels = mine.shape[1], mine.shape[2]
    block = 64

    def step(i, sums):
        rows = pl.ds(pl.multiple_of(i * block, block), block)
        at = pl.ds(pl.multiple_of(place[0] * half + i * block, block), block)
        turned_i = sign[0] * (other[0, rows, :] * mine[1, rows, :] - other[1, rows, :] * mine[0, rows, :])
        pro_r = other[0, rows, :] * mine[0, rows, :] + other[1, rows, :] * mine[1, rows, :]
        product[0, rows, :] = pro_r
        product[1, rows, :] = turned_i
        return add_sums(sums, pro_r, turned_i, phase_turn[0, at, :], phase_turn[1, at, :])

    zero = jnp.zeros((8, pixels), jnp.float32)
    sums = lax.fori_loop(0, half // block, step, (zero, zero, zero))
    for i, value in enumerate(totals(sums, pixels)):
        sums_out[i] = jnp.broadcast_to(value, sums_out.shape[1:])


def final_kernel(
    place, own, other, even, returned, phase_turn, shared, sums_here, sums_there,
    matrix, turned, turn, turn_in, turn_out, cos_part, sin_part, sent_r, sent_i, far_r, far_i, mixed, product, kept_r, kept_i, sems,
):
    pixels = returned.shape[1]
    columns_part(
        own, other, matrix, turned, turn_in, turn_out, cos_part, sin_part, 1, mixed
    )

    zero = jnp.zeros((8, pixels), jnp.float32)
    sums = (zero, zero, zero)
    for i in range(pixels // WIDE):
        rows = pl.ds(i * WIDE, WIDE)
        real, imag = even_and_odd(even, mixed, turned, turn, rows)
        sums = product_part(real, imag, returned, phase_turn, product, rows, sums)
    weight_r, weight_i = weight_of(*totals(sums, pixels))
    shared_r, shared_i = weight_of(
        *(sums_here[i, 0:1, 0:1] + sums_there[i, 0:1, 0:1] for i in range(3))
    )
    part = pixels // 4

    for out_r, out_i, core in ((kept_r, kept_i, place[0]), (sent_r, sent_i, 1 - place[0])):
        for s in range(2):

            here = jnp.where(place[0] == s, 1.0, 0.0)
            other_r, other_i = shared_r * here, shared_i * here

            def apply(i, carry, s=s, out_r=out_r, out_i=out_i, core=core, other_r=other_r, other_i=other_i):
                rows = pl.ds(pl.multiple_of((2 * s + core) * part + i * 32, 32), 32)
                at = pl.ds(pl.multiple_of(core * part + i * 32, 32), 32)
                to = pl.ds(pl.multiple_of(i * 32, 32), 32)
                pro_r, pro_i = product[0, rows, :], product[1, rows, :]
                sha_r, sha_i = shared[0, at, :], shared[1, at, :]
                out_r[s, to, :] = (weight_r * pro_r - weight_i * pro_i) + (
                    other_r * sha_r - other_i * sha_i
                )
                out_i[s, to, :] = (weight_r * pro_i + weight_i * pro_r) + (
                    other_r * sha_i + other_i * sha_r
                )
                return carry

            lax.fori_loop(0, part // 32, apply, 0)
        if out_r is kept_r:
            leaving = [
                pltpu.make_async_copy(kept_r, far_r, sems.at[0]),
                pltpu.make_async_copy(kept_i, far_i, sems.at[1]),
            ]
            for copy in leaving:
                copy.start()
    for copy in leaving:
        copy.wait()


def in_vmem(count):
    return [pl.BlockSpec(memory_space=pltpu.VMEM) for _ in range(count)]


def in_smem():
    return pl.BlockSpec(memory_space=pltpu.SMEM)


def limit(mebibytes):
    return pltpu.CompilerParams(vmem_limit_bytes=mebibytes * 1024 * 1024)


ROWS_LIMIT = 24
FIELD_LIMIT = 30
FINAL_LIMIT = 20


def far(value):
    return pltpu.with_memory_space_constraint(value, pltpu.HBM)


def rows_call(index, sources, plan, matrix, turn, bring=False):
    _, _, rows, pixels = sources[0].shape
    half = pixels // 2
    whole = jax.ShapeDtypeStruct((2, 2, rows, half), jnp.float32)
    part = jax.ShapeDtypeStruct((2, rows, half), jnp.float32)
    shapes = [shape for _, joined in plan for shape in ([whole] if joined else [part, part])]
    count = len(sources)

    def kernel(index, *refs):
        fields, refs = refs[:count], refs[count:]
        matrix, turn, refs = refs[0], refs[1], refs[2:]
        outs, scratch = list(refs[: len(shapes)]), refs[len(shapes) :]
        brought = []
        if bring:
            near_matrix, near_turn, table_sems = scratch[2:]
            brought = [
                pltpu.make_async_copy(turn, near_turn, table_sems.at[0]),
                pltpu.make_async_copy(matrix, near_matrix, table_sems.at[1]),
            ]
            matrix, turn = near_matrix, near_turn
        entries = []
        for at, (source, joined) in enumerate(plan):
            if joined:
                out = outs.pop(0)
                entries.append((fields[source], at, out.at[0], out.at[1]))
            else:
                entries.append((fields[source], at, outs.pop(0), outs.pop(0)))
        rows_kernel(entries, brought, index, matrix, turn, scratch[0], scratch[1])

    blocks = 2 * len(plan)
    scratch = [
        pltpu.VMEM((blocks, 2, rows // 2, pixels), jnp.float32),
        pltpu.SemaphoreType.DMA((blocks,)),
    ]
    table_specs = in_vmem(2)
    if bring:
        table_specs = [pl.BlockSpec(memory_space=pltpu.HBM)] * 2
        scratch += [
            pltpu.VMEM(matrix.shape, matrix.dtype),
            pltpu.VMEM(turn.shape, turn.dtype),
            pltpu.SemaphoreType.DMA((2,)),
        ]
        matrix, turn = far(matrix), far(turn)
    return pl.pallas_call(
        kernel,
        out_shape=tuple(shapes),
        in_specs=[in_smem()] + [pl.BlockSpec(memory_space=pltpu.HBM)] * count + table_specs,
        out_specs=tuple(in_vmem(len(shapes))),
        scratch_shapes=scratch,
        compiler_params=limit(ROWS_LIMIT),
        name="rows",
    )(index, *[far(source) for source in sources], matrix, turn)


def field_tables(tables):
    names = ("matrix", "turned", "turn", "turn_in", "turn_out", "cos_even", "sin_even", "cos_odd", "sin_odd")
    return [tables[name] for name in names]


def back_call(own, other, tables):
    half = own.shape[2]
    return pl.pallas_call(
        back_kernel,
        out_shape=jax.ShapeDtypeStruct((2, 2 * half, 2 * half), jnp.float32),
        in_specs=in_vmem(11),
        out_specs=in_vmem(1)[0],
        scratch_shapes=[pltpu.VMEM((2, 2, 2 * half, half), jnp.float32)],
        compiler_params=limit(FIELD_LIMIT),
        name="back",
    )(own, other, *field_tables(tables))


def even_call(own, other, tables):
    half = own.shape[1]
    return pl.pallas_call(
        even_kernel,
        out_shape=jax.ShapeDtypeStruct((2, 2 * half, half), jnp.float32),
        in_specs=in_vmem(8),
        out_specs=in_vmem(1)[0],
        scratch_shapes=[pltpu.VMEM((2, 2 * half, half), jnp.float32)],
        compiler_params=limit(FIELD_LIMIT),
        name="even",
    )(own, other, tables["matrix"], tables["turned"], tables["turn_in"],
      tables["turn_out"], tables["cos_even"], tables["sin_even"])


def shared_call(place, sign, own, other, tables):
    half = own.shape[2]
    part = jax.ShapeDtypeStruct((2, half, 2 * half), jnp.float32)
    return pl.pallas_call(
        shared_kernel,
        out_shape=(part, part),
        in_specs=[in_smem()] * 2 + in_vmem(11),
        out_specs=tuple(in_vmem(2)),
        scratch_shapes=[pltpu.VMEM((2, 2, 2 * half, half), jnp.float32)],
        compiler_params=limit(FIELD_LIMIT),
        name="shared",
    )(place.reshape(1), sign.reshape(1), own, other, *field_tables(tables))


def product_call(place, sign, mine, other, phase_turn):
    return pl.pallas_call(
        product_kernel,
        out_shape=(
            jax.ShapeDtypeStruct(mine.shape, jnp.float32),
            jax.ShapeDtypeStruct((3, 8, 128), jnp.float32),
        ),
        in_specs=[in_smem()] * 2 + in_vmem(3),
        out_specs=tuple(in_vmem(2)),
        compiler_params=limit(ROWS_LIMIT),
        name="product",
    )(place.reshape(1), sign.reshape(1), mine, other, phase_turn)


def final_call(place, own, other, even, returned, phase_turn, shared, sums_here, sums_there, tables):
    pixels = returned.shape[1]
    part = jax.ShapeDtypeStruct((2, pixels // 4, pixels), jnp.float32)
    return pl.pallas_call(
        final_kernel,
        out_shape=(part,) * 2 + (pltpu.HBM(part.shape, part.dtype),) * 2,
        in_specs=[in_smem()] + in_vmem(15),
        out_specs=tuple(in_vmem(2)) + (pl.BlockSpec(memory_space=pltpu.HBM),) * 2,
        scratch_shapes=[
            pltpu.VMEM(even.shape, jnp.float32),
            pltpu.VMEM(returned.shape, jnp.float32),
            pltpu.VMEM(part.shape, part.dtype),
            pltpu.VMEM(part.shape, part.dtype),
            pltpu.SemaphoreType.DMA((2,)),
        ],
        compiler_params=limit(FINAL_LIMIT),
        name="final",
    )(place.reshape(1), own, other, even, returned, phase_turn, shared, sums_here, sums_there, tables["matrix"], tables["turned"],
      tables["turn"], tables["turn_in"], tables["turn_out"], tables["cos_odd"], tables["sin_odd"])


def circle(turns):
    quarters = 4.0 * turns
    nearest = jnp.round(quarters)
    angle = (quarters - nearest) * (0.5 * math.pi)
    square = angle * angle
    sin = 1.0 / 362880.0
    for term in (-1.0 / 5040.0, 1.0 / 120.0, -1.0 / 6.0, 1.0):
        sin = sin * square + term
    sin = sin * angle
    cos = -1.0 / 3628800.0
    for term in (1.0 / 40320.0, -1.0 / 720.0, 1.0 / 24.0, -0.5, 1.0):
        cos = cos * square + term
    count = nearest.astype(jnp.int32)
    swapped = (count & 1) == 1
    cos, sin = jnp.where(swapped, sin, cos), jnp.where(swapped, cos, sin)
    cos = jnp.where(((count + 1) & 2) == 2, -cos, cos)
    sin = jnp.where((count & 2) == 2, -sin, sin)
    return cos, sin


def turned_table(half):
    index = jnp.arange(half, dtype=jnp.int32)
    wrapped = index[:, None] * index[None, :] % half
    cos, sin = circle(wrapped.astype(jnp.float32) / half)
    value = jnp.concatenate(
        [jnp.concatenate([cos, sin], axis=1), jnp.concatenate([-sin, cos], axis=1)], axis=0
    )
    high = lax.reduce_precision(value, 8, 7)
    return jnp.stack([high.astype(jnp.bfloat16), (value - high).astype(jnp.bfloat16)])


def permuted_transfer(pixels, e):
    half = pixels // 2
    order = jnp.arange(2, dtype=jnp.int32)[:, None] + 2 * jnp.arange(half, dtype=jnp.int32)[None, :]
    signed = jnp.where(order < half, order, order - pixels).astype(jnp.float32)
    squared = signed[:, :, None] ** 2 + signed[e][None, None, :] ** 2
    scaled = squared * (wavelength / (pixels * pixel_pitch)) ** 2
    cos, sin = circle(-(gap_length / wavelength) * scaled / (1.0 + jnp.sqrt(1.0 - scaled)))
    return cos / (pixels * pixels), sin / (pixels * pixels)


def after(value, *others):
    return lax.optimization_barrier((value,) + others)[0]


def whole_modes(forward_fields, backward_fields, phase):
    pixels = forward_fields.shape[3]
    half = pixels // 2
    modes_here = forward_fields.shape[1]
    mode_size = lax.axis_size("mode")
    outer = mode_size // 4
    axes = ("mode", "space")
    mode_index = lax.axis_index("mode")
    space_index = lax.axis_index("space")
    core_index = mode_index % 2
    x_index = mode_index // 2 % 2
    z_index = mode_index // 4

    def flat(mode, space):
        return mode * 2 + space

    everyone = [(mode, space) for mode in range(mode_size) for space in range(2)]
    to_space = [(flat(m, s), flat(m, 1 - s)) for m, s in everyone]
    to_core = [(flat(m, s), flat(m ^ 1, s)) for m, s in everyone]
    to_x = [(flat(m, s), flat(m ^ 2, s)) for m, s in everyone]
    to_z = {j: [(flat(m, s), flat(m ^ (4 * j), s)) for m, s in everyone] for j in range(1, outer)}

    def send(value, pairs):
        return lax.ppermute(value, axes, pairs)

    def swap_if(bit, value):
        return jnp.where(bit == 1, value[::-1], value)

    def by_z(value):
        shape = value.shape
        value = value.reshape((outer // 2, 2) + shape[1:])
        value = jnp.where(z_index % 2 == 1, value[:, ::-1], value)
        value = swap_if(z_index // 2, value)
        return value.reshape(shape)

    piece_rows = half // mode_size

    def share(value, bit, pairs):
        return swap_if(bit, jnp.stack([value, send(value, pairs)]))

    matrix = jnp.asarray(split_table(pixels))
    angle = 2.0 * np.pi / pixels * np.arange(half)
    turn = jnp.asarray(np.stack([np.cos(angle), np.sin(angle)]).astype(np.float32))

    last = jnp.full((), modes_here - 1, jnp.int32)
    both_fields = (backward_fields, forward_fields)
    (sent_backward,) = rows_call(
        (1 - space_index).reshape(1), (backward_fields,), ((0, True),), matrix, turn, True
    )
    got_backward = send(sent_backward, to_space)
    eighth = half // 8
    part = lax.dynamic_slice_in_dim(
        phase, after(core_index * 4 + x_index * 2 + z_index % 2, sent_backward) * eighth, eighth, axis=0
    )
    other_part = send(part, to_space)
    last_backward, last_forward = rows_call(
        after(jnp.stack([last, last]), part), both_fields, ((0, True), (1, True)), matrix, turn
    )
    core_backward = send(last_backward, to_core)
    modes = jnp.stack([1 - space_index])
    sent_even, sent_odd = rows_call(
        after(modes, last_backward), (forward_fields,), ((0, False),), matrix, turn
    )
    stays = core_index == space_index
    sent_shared = jnp.where(stays, core_backward, last_forward)
    got_shared = send(sent_shared, to_space)
    own_shared = jnp.where(stays, last_forward, core_backward)
    got_even = send(sent_even, to_space)
    got_odd = send(sent_odd, to_space)
    cos_even, sin_even = permuted_transfer(pixels, 0)
    cos_odd, sin_odd = permuted_transfer(pixels, 1)
    modes = jnp.stack([space_index, space_index])
    own_backward, own_even, own_odd = rows_call(
        after(modes, sent_odd, sent_shared), both_fields, ((0, True), (1, False)), matrix, turn
    )

    other_part = after(other_part, own_odd)
    other_phase = share(share(share(other_part, z_index % 2, to_z[1]), x_index, to_x), core_index, to_core)
    whole_phase = swap_if(
        space_index, jnp.stack([phase, other_phase.reshape(half, pixels)])
    ).reshape(pixels, pixels)
    phase_turn = jnp.stack(circle(whole_phase * (0.5 / math.pi)))

    turn_out = jnp.broadcast_to(turn[:, :, None], (2, half, 128))
    tables = {
        "matrix": matrix,
        "turned": turned_table(half),
        "turn": turn,
        "turn_out": turn_out,
        "turn_in": turn_out * (1.0 - 2.0 * space_index.astype(jnp.float32)),
        "cos_even": cos_even,
        "sin_even": sin_even,
        "cos_odd": cos_odd,
        "sin_odd": sin_odd,
    }

    sign = jnp.where(stays, 1.0, -1.0)
    returned = back_call(own_backward, got_backward, tables)
    give, mine = shared_call(core_index, sign, after(own_shared, returned), got_shared, tables)
    shared, sums_here = product_call(core_index, sign, mine, send(give, to_core), phase_turn)
    sums_there = send(sums_here, to_core)
    even = even_call(after(own_even, sums_here), got_even, tables)
    sent_r, sent_i, kept_r, kept_i = final_call(
        core_index, own_odd, got_odd, even, returned, phase_turn, shared, sums_here, sums_there, tables
    )
    shape = (2, 2, outer, piece_rows, pixels)

    def keep(value, axis, index):
        return lax.dynamic_index_in_dim(value, index, axis=axis, keepdims=False)

    def core_step(kept, sent, axis, index, pairs):
        kept, got = kept.reshape(shape), send(sent, to_core).reshape(shape)
        leaves = keep(kept, axis, 1 - index) + keep(got, axis, 1 - index)
        return keep(kept, axis, index) + keep(got, axis, index) + send(leaves, pairs)

    def step(value, axis, index, pairs):
        return keep(value, axis, index) + send(keep(value, axis, 1 - index), pairs)

    real = core_step(kept_r, sent_r, 1, x_index, to_x)
    imag = core_step(kept_i, sent_i, 0, space_index, to_space)
    real = step(real, 0, space_index, to_space)
    imag = step(imag, 0, x_index, to_x)
    both = by_z(jnp.stack([real, imag], axis=1))
    got = {j: send(both[j], to_z[j]) for j in range(1, outer)}
    total = both[0]
    for j in range(1, outer):
        total = total + got[j]
    mode_root = math.sqrt(modes_here * mode_size)
    place = (core_index * 2 + x_index) * outer + z_index
    piece = lax.dynamic_slice_in_dim(phase, place * piece_rows, piece_rows, axis=0)
    updated = phase_update(total[0] / mode_root, total[1] / mode_root, piece)
    got = {j: send(updated, to_z[j]) for j in range(1, outer)}
    pieces = by_z(jnp.stack([updated] + [got[j] for j in range(1, outer)]))
    pieces = share(share(pieces, x_index, to_x), core_index, to_core)
    return pieces.reshape(half, pixels)


def on_device(forward_fields, backward_fields, phase):
    pixels = forward_fields.shape[3]
    if (
        lax.axis_size("space") == 2
        and lax.axis_size("mode") == 16
        and forward_fields.shape[1] == 3
        and pixels % 512 == 0
    ):
        return whole_modes(forward_fields, backward_fields, phase)
    return split_planes(forward_fields, backward_fields, phase)


def solution(mesh):
    in_specs = (P(None, "mode", "space", None), P(None, "mode", "space", None), P("space", None))
    out_specs = P("space", None)
    return jax.shard_map(
        on_device, mesh=mesh, in_specs=in_specs, out_specs=out_specs, check_vma=False
    )
```
